512 devices in a mesh: tiles: 128 (over y, x, z_lo, core), slab: 4 (over z_hi).
Axes of the slice: x: 4, y: 4, z: 16 (z_hi: 4, z_lo: 4; z = z_hi * 4 + z_lo), core: 2. Of those that a mesh axis runs over, the one named last changes fastest.
Arguments:
- adjoint: float32 [4, 3, 512, 8100], P('slab', None, 'tiles'), may hold values from -6 to 6
- state: float32 [4, 3, 512, 8100], P('slab', None, 'tiles'), may hold values from 0.1 to 10
- weights: float32 [4, 512, 8100], P('slab', 'tiles'), may hold values from 0.02 to 0.24
- vertical: float32 [4, 512, 8100], P('slab', 'tiles'), may hold values from 0.02 to 0.3
- mask: int32 [4, 512, 8100], P('slab', 'tiles'), may hold values 0 or 1
- rate: float32 [3, 512, 8100], P(None, 'tiles'), may hold values from 0.005 to 0.1
- neighbours: int32 [512, 4], P('tiles'), may hold values from -1 to 511, as said below
- links: int32 [512, 4], P('tiles'), may hold values from 0 to 7, as said below
- owners: int32 [512], replicated, may hold values from 0 to 127
Outputs:
- adjoint_out: float32 [4, 3, 512, 8100], P('slab', None, 'tiles')
- control_gradient: float32 [4, 128, 675], P('slab', 'tiles')
The draws below stay inside these ranges and needn't reach their ends.
Inputs may be any that keep to these rules, and one draw needn't show every extreme that they name: Tiles are placed row by row in a layout of 8 columns, tile t at position t + 2: neighbours[t, s] is t - 8, t + 8, t - 1, t + 1 or -1, and links are mutual: if neighbours[t, s] = u >= 0 then neighbours[u, links[t, s] // 2] = t and links[u, links[t, s] // 2] = 2 s + links[t, s] % 2. `links`: 0 where the side is closed; odd only across the seam between the faces and the cap.
All inputs are finite; a program needn't handle non-finite values. No bound on the sum of `mask` on one device may be relied on, other than what follows from the above.
Results may differ from the reference program's by a relative error of at most 0.000071.
Values sent between devices are 32-bit elements; how exact they have to be, the bound alone decides.
A program may use at most 64 MiB of HBM per device.

```python
import math
import jax
import jax.numpy as jnp
from jax import lax

TILE = 90
TRACERS = 3
LEVELS = 4
SUBSTEPS = 2
BLOCK = 6
ROW_TILES = 8
TILES_DEV = 4
TILES_ALL = 512
COARSE = 15
OWNERS = 128


def tile_layout(key):
    rows = (TILES_ALL + 2 + ROW_TILES - 1) // ROW_TILES
    first, second, third = jax.random.split(jax.random.fold_in(key, 11), 3)
    shut_across = jax.random.randint(first, (rows, ROW_TILES - 1), 0, 2) == 0
    shut_along = jax.random.randint(second, (max(rows - 1, 1), ROW_TILES), 0, 2) == 0
    seam = jax.random.randint(third, (), 3, 7).astype(jnp.int32)
    index = jnp.arange(TILES_ALL, dtype=jnp.int32)
    position = index + 2
    row_of = position // ROW_TILES
    col_of = position % ROW_TILES
    turned = col_of >= seam
    drawn_dr = jnp.array([-1, 1, 0, 0], jnp.int32)
    drawn_dc = jnp.array([0, 0, -1, 1], jnp.int32)
    turned_dr = jnp.array([0, 0, 1, -1], jnp.int32)
    turned_dc = jnp.array([-1, 1, 0, 0], jnp.int32)
    step_r = jnp.where(turned[:, None], turned_dr[None, :], drawn_dr[None, :])
    step_c = jnp.where(turned[:, None], turned_dc[None, :], drawn_dc[None, :])
    near_r = row_of[:, None] + step_r
    near_c = col_of[:, None] + step_c
    near_pos = near_r * ROW_TILES + near_c
    inside = (near_r >= 0) & (near_r < rows) & (near_c >= 0) & (near_c < ROW_TILES)
    inside = inside & (near_pos >= 2) & (near_pos < TILES_ALL + 2)
    edge_c = jnp.clip(jnp.minimum(col_of[:, None], near_c), 0, ROW_TILES - 2)
    edge_r = jnp.clip(jnp.minimum(row_of[:, None], near_r), 0, max(rows - 2, 0))
    row_here = jnp.broadcast_to(row_of[:, None], edge_c.shape)
    col_here = jnp.broadcast_to(col_of[:, None], edge_c.shape)
    closed = jnp.where(step_r == 0, shut_across[row_here, edge_c], shut_along[edge_r, col_here])
    target = near_pos - 2
    middle = TILES_ALL // 2
    own_middle = (index >= middle) & (index < middle + TILES_DEV)
    touches = own_middle[:, None] | (target >= middle) & (target < middle + TILES_DEV)
    middle_row = (middle + 2) // ROW_TILES
    seam_edge = (step_r == 0) & (row_here == middle_row) & (edge_c == seam - 1)
    opened = inside & (jnp.logical_not(closed) | touches | seam_edge)
    back_r = -step_r
    back_c = -step_c
    near_turned = near_c >= seam
    drawn_side = jnp.where(back_r == -1, 0, jnp.where(back_r == 1, 1, jnp.where(back_c == -1, 2, 3)))
    turned_side = jnp.where(back_c == -1, 0, jnp.where(back_c == 1, 1, jnp.where(back_r == 1, 2, 3)))
    back_side = jnp.where(near_turned, turned_side, drawn_side)
    flipped = (near_turned != turned[:, None]).astype(jnp.int32)
    neighbours = jnp.where(opened, target, -1).astype(jnp.int32)
    links = jnp.where(opened, back_side * 2 + flipped, 0).astype(jnp.int32)
    return (neighbours, links)


def draw_neighbours(key, part):
    return tile_layout(key)[0]


def draw_links(key, part):
    return tile_layout(key)[1]


def touch_ends(result, rng, low, top_value):
    longest = result.shape.index(max(result.shape))
    spots = []
    for shift in (0, 1):
        where = [jax.random.randint(jax.random.fold_in(rng, axis), (), 0, length) for axis, length in enumerate(result.shape)]
        where[longest] = (where[longest] + shift) % result.shape[longest]
        spots.append(tuple(where))
    return result.at[spots[0]].set(low).at[spots[1]].set(top_value)


def block_scale(rng, dims, shards, smallest, largest):
    loudness = 1.0
    for dim, shards_of in shards:
        steps = jax.random.uniform(jax.random.fold_in(jax.random.fold_in(rng, 6), dim), (shards_of,), jnp.float32, smallest / len(shards), largest / len(shards))
        loudness = loudness * jnp.repeat(jnp.exp(steps), dims[dim] // shards_of).reshape((-1,) + (1,) * (len(dims) - 1 - dim))
    return loudness


def bell_draw(stream_key, dims, deviation, most, cuts=(), kind=jnp.bfloat16):
    drawn = deviation * jax.random.normal(stream_key, dims, jnp.float32)
    if cuts:
        drawn = drawn * block_scale(stream_key, dims, cuts, -0.22, 0.18)
    return jnp.clip(drawn, -most, most).astype(kind)


def setup_inputs(seed: int = 0) -> dict:
    streams_of = jax.random.split(jax.random.key(seed), 10)
    return {
        "adjoint": bell_draw(streams_of[0], (LEVELS, TRACERS, TILES_ALL, TILE * TILE), 1.0, 6.0, ((0, 4), (2, 128)), jnp.float32),
        "state": jnp.clip(jnp.exp(math.log(10.0) - 4.6051702 * jax.random.uniform(streams_of[1], (LEVELS, TRACERS, TILES_ALL, TILE * TILE), jnp.float32) ** block_scale(streams_of[1], (LEVELS, TRACERS, TILES_ALL, TILE * TILE), ((0, 4), (2, 128)), -0.2, 0.2)), 0.1, 10.0),
        "weights": jnp.clip(jnp.exp(math.log(0.24) - 2.4849066 * jax.random.uniform(streams_of[2], (LEVELS, TILES_ALL, TILE * TILE), jnp.float32) ** block_scale(streams_of[2], (LEVELS, TILES_ALL, TILE * TILE), ((0, 4), (1, 128)), -0.2, 0.2)), 0.02, 0.24),
        "vertical": jnp.clip(jnp.exp(math.log(0.3) - 2.7080503 * jax.random.uniform(streams_of[3], (LEVELS, TILES_ALL, TILE * TILE), jnp.float32) ** block_scale(streams_of[3], (LEVELS, TILES_ALL, TILE * TILE), ((0, 4), (1, 128)), -0.2, 0.2)), 0.02, 0.3),
        "mask": touch_ends((jax.random.randint(streams_of[4], (LEVELS, TILES_ALL, TILE * TILE), 0, 4) < 3).astype(jnp.int32), jax.random.fold_in(streams_of[4], 1), 0, 1),
        "rate": jnp.clip(jnp.exp(math.log(0.1) - 2.9957323 * jax.random.uniform(streams_of[5], (TRACERS, TILES_ALL, TILE * TILE), jnp.float32) ** block_scale(streams_of[5], (TRACERS, TILES_ALL, TILE * TILE), ((1, 128),), -0.2, 0.2)), 0.005, 0.1),
        "neighbours": draw_neighbours(jax.random.fold_in(streams_of[9], 71), 0),
        "links": draw_links(jax.random.fold_in(streams_of[9], 71), 0),
        "owners": touch_ends(jax.random.randint(streams_of[8], (TILES_ALL,), 0, OWNERS), jax.random.fold_in(streams_of[8], 1), 0, OWNERS - 1).astype(jnp.int32),
    }


def edge_rows(field):
    return jnp.concatenate((field[..., 0, :], field[..., -1, :], field[..., :, 0], field[..., :, -1]), axis=-1)


def pick_halo(edge_all, neighbours, links):
    width = edge_all.shape[-1] // 4
    grid = edge_all.reshape(edge_all.shape[:-1] + (4, width))
    source = jnp.maximum(neighbours, 0)
    picked = grid[..., source, links // 2, :]
    picked = jnp.where((links % 2)[..., None] == 1, picked[..., ::-1], picked)
    return jnp.where(neighbours[..., None] >= 0, picked, jnp.float32(0.0))


def neighbour_sum(field, halo):
    upper = jnp.concatenate((halo[..., 0, :][..., None, :], field[..., :-1, :]), axis=-2)
    lower = jnp.concatenate((field[..., 1:, :], halo[..., 1, :][..., None, :]), axis=-2)
    left_side = jnp.concatenate((halo[..., 2, :][..., :, None], field[..., :, :-1]), axis=-1)
    right_side = jnp.concatenate((field[..., :, 1:], halo[..., 3, :][..., :, None]), axis=-1)
    return upper + lower + left_side + right_side


def reference(adjoint, state, weights, vertical, mask, rate, neighbours, links, owners):
    count_all = adjoint.shape[2]
    shape_four = (LEVELS, count_all, TILE, TILE)
    lam = adjoint.reshape(LEVELS, TRACERS, count_all, TILE, TILE)
    wet = mask.astype(jnp.float32).reshape(shape_four)
    mixing = wet * weights.reshape(shape_four)
    count = neighbour_sum(wet, pick_halo(edge_rows(wet), neighbours, links))
    zero_level = jnp.zeros((1, count_all, TILE, TILE), jnp.float32)
    wet_above = jnp.concatenate((zero_level, wet[:-1]), axis=0)
    above = vertical.reshape(shape_four) * wet * wet_above
    below = jnp.concatenate((above[1:], zero_level), axis=0)
    uptake = 1.0 - rate.reshape(1, TRACERS, count_all, TILE, TILE)
    zero_tracers = jnp.zeros((1, TRACERS, count_all, TILE, TILE), jnp.float32)
    for step in range(SUBSTEPS):
        spread = mixing[:, None] * lam
        halo = pick_halo(edge_rows(spread), neighbours, links)
        horizontal = lam * (1.0 - (mixing * count)[:, None]) + wet[:, None] * neighbour_sum(spread, halo)
        taken = horizontal * uptake
        from_above = jnp.concatenate((zero_tracers, taken[:-1]), axis=0)
        from_below = jnp.concatenate((taken[1:], zero_tracers), axis=0)
        lam = taken + above[:, None] * (from_above - taken) + below[:, None] * (from_below - taken)
    term = wet[:, None] * lam * state.reshape(LEVELS, TRACERS, count_all, TILE, TILE)
    term = term.reshape(LEVELS, TRACERS, count_all, COARSE, BLOCK, COARSE, BLOCK).sum(axis=(4, 6))
    onehot = (owners[:, None] == jnp.arange(OWNERS, dtype=jnp.int32)[None, :]).astype(jnp.float32)
    gradient = jnp.einsum("lctyx,tk->lkcyx", term, onehot, precision=lax.Precision.HIGHEST)
    return lam.reshape(LEVELS, TRACERS, count_all, TILE * TILE), gradient.reshape(LEVELS, OWNERS, TRACERS * COARSE * COARSE)
```

```python
import jax
import jax.numpy as jnp
from jax import lax
from jax.experimental import pallas as pl
from jax.experimental.pallas import tpu as pltpu
from jax.sharding import PartitionSpec as P

TILE = 90
CELLS = TILE * TILE
SUBSTEPS = 2
BLOCK = 6
COARSE = 15
LANES = 128
ROWS = 64
LEVELS = 4
TRACERS = 3
FULL = LEVELS * ROWS
TAIL = CELLS - (ROWS - 1) * LANES
MESH = pl.DeviceIdType.MESH
FIELDS = 5
LAM = (1, 3, 4)
NEAR = 8
FAR = 16


def iota(shape, dim):
    return lax.broadcasted_iota(jnp.int32, shape, dim)


def shifted(field, distance):
    rows = field.shape[0]
    lane = iota(field.shape, 1)
    down, over = divmod(distance, LANES)
    turned = pltpu.roll(field, (LANES - over) % LANES, 1)
    near = pltpu.roll(turned, (-down) % rows, 0) if down % rows else turned
    far = pltpu.roll(turned, (-down - 1) % rows, 0) if (down + 1) % rows else turned
    return jnp.where(lane >= LANES - over, far, near)


def pieces(value):
    high = value.astype(jnp.bfloat16)
    rest = value - high.astype(jnp.float32)
    middle = rest.astype(jnp.bfloat16)
    low = (rest - middle.astype(jnp.float32)).astype(jnp.bfloat16)
    return high, middle, low


def pick(value, onehot):
    high, middle, low = pieces(value)
    return (
        jnp.dot(high, onehot, preferred_element_type=jnp.float32)
        + jnp.dot(middle, onehot, preferred_element_type=jnp.float32)
        + jnp.dot(low, onehot, preferred_element_type=jnp.float32)
    )


def spread_rows(rows):
    return jnp.concatenate(
        [jnp.broadcast_to(rows[l : l + 1], (ROWS, LANES)) for l in range(LEVELS)], axis=0
    )


def kernel(
    adjoint, state, weights, vertical, mask, rate, neighbours, links, owners,
    out, gradient,
    mine, column, uptake, forward, wet_rows, above_rows, below_rows, keep_rows,
    lam_rows, gather_side, mask_side, place_side, gather_block, mask_block,
    edge_out, edge_in, back_out, back_in, block_own, block_all, part, part_in,
    send_field, recv_field, send_edge, recv_edge, send_back, recv_back,
    send_near, recv_near, send_far, recv_far,
):
    here = lax.axis_index("tiles")
    slab = lax.axis_index("slab")
    tiles = lax.axis_size("tiles")
    core = here % 2
    depth = (here // 2) % 4
    across = (here // 8) % 4
    along = here // 32

    def slab_peer(k):
        return here, (slab + k) % LEVELS

    def beside(n):
        if n == 0:
            return (here + tiles - 2) % tiles, slab
        if n == 1:
            return (here + 2) % tiles, slab
        if n == 2:
            gone = (slab == 0).astype(jnp.int32)
            return (here + tiles - gone) % tiles, (slab + LEVELS - 1) % LEVELS
        gone = (slab == LEVELS - 1).astype(jnp.int32)
        return (here + gone) % tiles, (slab + 1) % LEVELS

    near_me = across * 2 + core
    far_me = along * 4 + depth

    def near_peer(k):
        other = (near_me + k) % NEAR
        return along * 32 + (other // 2) * 8 + depth * 2 + other % 2, slab

    def far_peer(k):
        other = (far_me + k) % FAR
        return (other // 4) * 32 + across * 8 + (other % 4) * 2 + core, slab

    barrier = pltpu.get_barrier_semaphore()
    peers = (
        [slab_peer(k) for k in range(1, LEVELS)]
        + [beside(n) for n in range(4)]
        + [near_peer(k) for k in range(1, NEAR)]
        + [far_peer(k) for k in range(1, FAR)]
    )
    for peer in peers:
        pl.semaphore_signal(barrier, inc=1, device_id=peer, device_id_type=MESH)

    small = iota((4, LANES), 1) < TAIL

    def last(ref, *lead):
        tail = ref[(*lead, slice(None), slice(CELLS - LANES, CELLS))]
        return jnp.where(small, pltpu.roll(tail, TAIL, 1), jnp.zeros_like(tail))

    def load_all(start, read, read_last, target):
        def body(k, carry):
            target[pl.ds(start + k, 4, stride=ROWS), :] = read(pl.ds(pl.multiple_of(k * LANES, LANES), LANES))
            return carry

        lax.fori_loop(0, ROWS - 1, body, 0)
        target[pl.ds(start + ROWS - 1, 4, stride=ROWS), :] = read_last()

    def wet_of(value):
        return value.astype(jnp.float32)

    load_all(
        0,
        lambda at: wet_of(mask[0, :, at]) * weights[0, :, at],
        lambda: wet_of(last(mask, 0)) * last(weights, 0),
        mine,
    )
    load_all(LAM[0] * FULL, lambda at: adjoint[0, 0, :, at], lambda: last(adjoint, 0, 0), mine)
    load_all(
        2 * FULL,
        lambda at: wet_of(mask[0, :, at]) * vertical[0, :, at],
        lambda: wet_of(last(mask, 0)) * last(vertical, 0),
        mine,
    )
    for c in (1, 2):
        load_all(
            LAM[c] * FULL,
            lambda at, c=c: adjoint[0, c, :, at],
            lambda c=c: last(adjoint, 0, c),
            mine,
        )

    pl.semaphore_wait(barrier, len(peers))

    def row_of(f, which):
        return pl.ds(pl.multiple_of(f * FULL + which * ROWS, ROWS), ROWS)

    def field_copy(f, k):
        to = slab_peer(k)
        return pltpu.make_async_remote_copy(
            src_ref=mine.at[row_of(f, to[1])],
            dst_ref=column.at[row_of(f, slab)],
            send_sem=send_field.at[f, k],
            recv_sem=recv_field.at[f, k],
            device_id=to,
            device_id_type=MESH,
        )

    for f in range(FIELDS):
        for k in (1, 3, 2):
            field_copy(f, k).start()
        column[row_of(f, slab), :] = mine[row_of(f, slab), :]

    position = iota((LANES, 2 * LANES), 1)
    y = position % LANES
    cell = TILE * y + jnp.where(position < LANES, 0, TILE - 1)
    lane = iota((LANES, 2 * LANES), 0)
    gather_side[...] = ((cell % LANES == lane) & (y < TILE)).astype(jnp.bfloat16)
    position = iota((ROWS, 2 * LANES), 1)
    y = position % LANES
    cell = TILE * y + jnp.where(position < LANES, 0, TILE - 1)
    mask_side[...] = ((cell // LANES == iota((ROWS, 2 * LANES), 0)) & (y < TILE)).astype(jnp.float32)
    position = iota((2 * LANES, LANES), 0)
    y = position % LANES
    cell = TILE * y + jnp.where(position < LANES, 0, TILE - 1)
    place_side[...] = ((cell % LANES == iota((2 * LANES, LANES), 1)) & (y < TILE)).astype(jnp.bfloat16)
    position = iota((LANES, 2 * LANES), 1)
    cell = BLOCK * TILE * (position // COARSE) + BLOCK * (position % COARSE)
    gather_block[...] = (
        (cell % LANES == iota((LANES, 2 * LANES), 0)) & (position < COARSE * COARSE)
    ).astype(jnp.bfloat16)
    position = iota((ROWS, 2 * LANES), 1)
    cell = BLOCK * TILE * (position // COARSE) + BLOCK * (position % COARSE)
    mask_block[...] = (
        (cell // LANES == iota((ROWS, 2 * LANES), 0)) & (position < COARSE * COARSE)
    ).astype(jnp.float32)
    turn = (iota((LANES, LANES), 0) + iota((LANES, LANES), 1) == TILE - 1).astype(jnp.bfloat16)

    flat = (iota((FULL, LANES), 0) % ROWS) * LANES + iota((FULL, LANES), 1)
    in_row = flat % TILE
    first_row = flat < TILE
    final_row = flat >= CELLS - TILE
    forward[0:FULL] = (in_row != 0).astype(jnp.float32)
    forward[FULL : 2 * FULL] = (in_row != TILE - 1).astype(jnp.float32)

    for c in range(TRACERS):
        load_all(c * FULL, lambda at, c=c: 1.0 - rate[c, :, at], lambda c=c: 1.0 - last(rate, c), uptake)

    tile = here * 4 + slab
    code, turned = [], []
    for side in range(4):
        to = jnp.full((LEVELS, LANES), neighbours[slab, side], jnp.int32)
        link = jnp.full((LEVELS, LANES), links[slab, side], jnp.int32)
        slot = jnp.where(
            to == tile - 8, 0, jnp.where(to == tile + 8, 4, jnp.where(to == tile - 1, 8, 12))
        )
        code.append(jnp.where(to < 0, -1, slot + lax.shift_right_logical(link, 1)))
        turned.append((link & 1) == 1)

    lane4 = iota((LEVELS, LANES), 1)

    def edges_of(field):
        top = jnp.concatenate([field[l * ROWS : l * ROWS + 1] for l in range(LEVELS)], axis=0)
        one = jnp.concatenate([field[l * ROWS + 62 : l * ROWS + 63] for l in range(LEVELS)], axis=0)
        two = jnp.concatenate([field[l * ROWS + 63 : l * ROWS + 64] for l in range(LEVELS)], axis=0)
        low = jnp.where(lane4 < 54, pltpu.roll(one, 54, 1), pltpu.roll(two, 54, 1))
        sides = pick(field, gather_side[...])
        chosen = mask_side[...]
        rows = jnp.concatenate(
            [
                jnp.sum(sides[l * ROWS : (l + 1) * ROWS] * chosen, axis=0, keepdims=True)
                for l in range(LEVELS)
            ],
            axis=0,
        )
        return top, low, rows[:, :LANES], rows[:, LANES:]

    def edge_copy(m, n):
        return pltpu.make_async_remote_copy(
            src_ref=edge_out.at[m],
            dst_ref=edge_in.at[m, n ^ 1],
            send_sem=send_edge.at[m, n],
            recv_sem=recv_edge.at[m, n ^ 1],
            device_id=beside(n),
            device_id_type=MESH,
        )

    def send_edges(m, field):
        for side, rows in enumerate(edges_of(field)):
            edge_out[m, side * LEVELS : (side + 1) * LEVELS, :] = rows
        for n in range(4):
            edge_copy(m, n).start()

    def halo(m):
        for n in range(4):
            edge_copy(m, n ^ 1).wait_recv()
        found = []
        for side in range(4):
            value = jnp.zeros((LEVELS, LANES), jnp.float32)
            for n in range(4):
                for other in range(4):
                    value = jnp.where(
                        code[side] == n * 4 + other,
                        edge_in[m, n, other * LEVELS : (other + 1) * LEVELS, :],
                        value,
                    )
            found.append(value)
        back = pick(jnp.concatenate(found, axis=0), turn)
        return [
            jnp.where(turned[side], back[side * LEVELS : (side + 1) * LEVELS], found[side])
            for side in range(4)
        ]

    def neighbour_sum(field, m):
        top, low, left, right = halo(m)
        upper = jnp.where(first_row, spread_rows(top), shifted(field, -TILE))
        lower = jnp.where(final_row, spread_rows(pltpu.roll(low, 74, 1)), shifted(field, TILE))
        before = forward[0:FULL] * shifted(field, -1)
        after = forward[FULL : 2 * FULL] * shifted(field, 1)
        chosen = mask_side[...]
        both = jnp.concatenate([left, right], axis=1)
        placed = jnp.concatenate([chosen * both[l : l + 1] for l in range(LEVELS)], axis=0)
        return upper + lower + before + after + pick(placed, place_side[...])

    def arrived(f):
        for k in range(1, LEVELS):
            field_copy(f, k).wait_recv()

    def back_copy(c, k):
        to = slab_peer(k)
        return pltpu.make_async_remote_copy(
            src_ref=back_out.at[row_of(c, to[1])],
            dst_ref=back_in.at[row_of(c, slab)],
            send_sem=send_back.at[c, k],
            recv_sem=recv_back.at[c, k],
            device_id=to,
            device_id_type=MESH,
        )

    def fluxes(c, step):
        m = c * SUBSTEPS + step
        lam = column[LAM[c] * FULL : (LAM[c] + 1) * FULL] if step == 0 else lam_rows[...]
        mixing = column[0:FULL]
        moved = lam * keep_rows[...] + wet_rows[...] * neighbour_sum(mixing * lam, m)
        kept = uptake[row_of(c, slab), :]
        u = jnp.concatenate([moved[l * ROWS : (l + 1) * ROWS] * kept for l in range(LEVELS)], axis=0)
        up = pltpu.roll(u, ROWS, 0)
        down = pltpu.roll(u, FULL - ROWS, 0)
        return u + above_rows[...] * (up - u) + below_rows[...] * (down - u)

    def middle(c):
        lam = fluxes(c, 0)
        lam_rows[...] = lam
        send_edges(c * SUBSTEPS + 1, column[0:FULL] * lam)

    def ends(c):
        lam = fluxes(c, 1)
        back_out[c * FULL : (c + 1) * FULL] = lam
        for k in (1, 3, 2):
            back_copy(c, k).start()
        back_in[row_of(c, slab), :] = back_out[row_of(c, slab), :]

    def opens(c):
        arrived(LAM[c])
        send_edges(c * SUBSTEPS, column[0:FULL] * column[LAM[c] * FULL : (LAM[c] + 1) * FULL])

    arrived(0)
    wet = (column[0:FULL] > 0).astype(jnp.float32)
    wet_rows[...] = wet
    send_edges(TRACERS * SUBSTEPS, wet)
    opens(0)
    keep_rows[...] = 1.0 - column[0:FULL] * neighbour_sum(wet_rows[...], TRACERS * SUBSTEPS)
    arrived(2)
    wet = wet_rows[...]
    inner = iota((FULL, LANES), 0) >= ROWS
    above = jnp.where(inner, column[2 * FULL : 3 * FULL] * pltpu.roll(wet, ROWS, 0), 0.0)
    above_rows[...] = above
    below_rows[...] = pltpu.roll(above, FULL - ROWS, 0)
    middle(0)
    opens(1)
    ends(0)
    middle(1)
    opens(2)
    ends(1)
    middle(2)
    ends(2)

    wide = iota((4, LANES), 1)
    block_own[...] = jnp.zeros_like(block_own)
    for c in range(TRACERS):
        load_all(c * FULL, lambda at, c=c: state[0, c, :, at], lambda c=c: last(state, 0, c), forward_state(forward))
    for c in range(TRACERS):
        for k in range(1, LEVELS):
            back_copy(c, k).wait_recv()

        def body(k, carry, c=c):
            out[0, c, :, pl.ds(pl.multiple_of(k * LANES, LANES), LANES)] = back_in[
                pl.ds(c * FULL + k, 4, stride=ROWS), :
            ]
            return carry

        lax.fori_loop(0, ROWS - 1, body, 0)
        out[0, c, :, (ROWS - 1) * LANES : CELLS] = back_in[
            pl.ds(c * FULL + ROWS - 1, 4, stride=ROWS), :
        ][:, :TAIL]
        lam = back_in[c * FULL : (c + 1) * FULL]
        term = jnp.where(mine[0:FULL] > 0, lam, 0.0) * forward[(2 + c) * FULL : (3 + c) * FULL]
        three = term + shifted(term, 1) + shifted(term, 2)
        six = three + shifted(three, 3)
        three = six + shifted(six, TILE) + shifted(six, 2 * TILE)
        six = three + shifted(three, 3 * TILE)
        blocks = pick(six, gather_block[...])
        chosen = mask_block[...]
        for j in range(4):
            row = jnp.sum(blocks[j * ROWS : (j + 1) * ROWS] * chosen, axis=0, keepdims=True)
            block_own[8 * j + 2 * c : 8 * j + 2 * c + 1, :] = row[:, :LANES]
            block_own[8 * j + 2 * c + 1 : 8 * j + 2 * c + 2, :] = row[:, LANES:]

    def near_copy(k):
        return pltpu.make_async_remote_copy(
            src_ref=block_own,
            dst_ref=block_all.at[near_me],
            send_sem=send_near.at[k],
            recv_sem=recv_near.at[k],
            device_id=near_peer(k),
            device_id_type=MESH,
        )

    for k in range(1, NEAR):
        near_copy(k).start()
    block_all[near_me] = block_own[...]
    which = iota((8 * FAR, LANES), 0) // 8
    owner_of = (which // 4) * 32 + across * 8 + (which % 4) * 2 + core
    for k in range(1, NEAR):
        near_copy(k).wait_recv()

    def add(t, total):
        member = t // 4
        source = along * 32 + (member // 2) * 8 + depth * 2 + member % 2
        owner = jnp.full((8 * FAR, LANES), owners[source * 4 + t % 4], jnp.int32)
        rows = block_all[member, pl.ds(pl.multiple_of((t % 4) * 8, 8), 8), :]
        return total + jnp.where(owner == owner_of, jnp.concatenate([rows] * FAR, axis=0), 0.0)

    part[...] = lax.fori_loop(0, 4 * NEAR, add, jnp.zeros((8 * FAR, LANES), jnp.float32))

    def far_copy(k):
        other = (far_me + k) % FAR
        return pltpu.make_async_remote_copy(
            src_ref=part.at[pl.ds(pl.multiple_of(other * 8, 8), 8)],
            dst_ref=part_in.at[far_me],
            send_sem=send_far.at[k],
            recv_sem=recv_far.at[k],
            device_id=far_peer(k),
            device_id_type=MESH,
        )

    for k in range(1, FAR):
        far_copy(k).start()
    part_in[far_me] = part[pl.ds(pl.multiple_of(far_me * 8, 8), 8), :]
    for k in range(1, FAR):
        far_copy(k).wait_recv()
    total = part_in[0]
    for k in range(1, FAR):
        total = total + part_in[k]
    area = COARSE * COARSE
    for c in range(TRACERS):
        gradient[0, :, c * area : c * area + LANES] = total[2 * c : 2 * c + 1]
        gradient[0, :, c * area + LANES : (c + 1) * area] = total[2 * c + 1 : 2 * c + 2, : area - LANES]

    for f in range(FIELDS):
        for k in range(1, LEVELS):
            field_copy(f, k).wait_send()
    for m in range(TRACERS * SUBSTEPS + 1):
        for n in range(4):
            edge_copy(m, n).wait_send()
    for c in range(TRACERS):
        for k in range(1, LEVELS):
            back_copy(c, k).wait_send()
    for k in range(1, NEAR):
        near_copy(k).wait_send()
    for k in range(1, FAR):
        far_copy(k).wait_send()


def forward_state(ref):
    return ref.at[pl.ds(2 * FULL, TRACERS * FULL)]


def shards(adjoint, state, weights, vertical, mask, rate, neighbours, links, owners):
    vmem = pl.BlockSpec(memory_space=pltpu.VMEM)
    smem = pl.BlockSpec(memory_space=pltpu.SMEM)
    f32 = jnp.float32
    dma = pltpu.SemaphoreType.DMA
    edges = TRACERS * SUBSTEPS + 1
    return pl.pallas_call(
        kernel,
        out_shape=(
            jax.ShapeDtypeStruct(adjoint.shape, f32),
            jax.ShapeDtypeStruct((1, 1, TRACERS * COARSE * COARSE), f32),
        ),
        in_specs=[vmem] * 6 + [smem] * 3,
        out_specs=(vmem, vmem),
        scratch_shapes=[
            pltpu.VMEM((FIELDS * FULL, LANES), f32),
            pltpu.VMEM((FIELDS * FULL, LANES), f32),
            pltpu.VMEM((TRACERS * FULL, LANES), f32),
            pltpu.VMEM((5 * FULL, LANES), f32),
            pltpu.VMEM((FULL, LANES), f32),
            pltpu.VMEM((FULL, LANES), f32),
            pltpu.VMEM((FULL, LANES), f32),
            pltpu.VMEM((FULL, LANES), f32),
            pltpu.VMEM((FULL, LANES), f32),
            pltpu.VMEM((LANES, 2 * LANES), jnp.bfloat16),
            pltpu.VMEM((ROWS, 2 * LANES), f32),
            pltpu.VMEM((2 * LANES, LANES), jnp.bfloat16),
            pltpu.VMEM((LANES, 2 * LANES), jnp.bfloat16),
            pltpu.VMEM((ROWS, 2 * LANES), f32),
            pltpu.VMEM((edges, 4 * LEVELS, LANES), f32),
            pltpu.VMEM((edges, 4, 4 * LEVELS, LANES), f32),
            pltpu.VMEM((TRACERS * FULL, LANES), f32),
            pltpu.VMEM((TRACERS * FULL, LANES), f32),
            pltpu.VMEM((32, LANES), f32),
            pltpu.VMEM((NEAR, 32, LANES), f32),
            pltpu.VMEM((8 * FAR, LANES), f32),
            pltpu.VMEM((FAR, 8, LANES), f32),
            dma((FIELDS, LEVELS)),
            dma((FIELDS, LEVELS)),
            dma((edges, 4)),
            dma((edges, 4)),
            dma((TRACERS, LEVELS)),
            dma((TRACERS, LEVELS)),
            dma((NEAR,)),
            dma((NEAR,)),
            dma((FAR,)),
            dma((FAR,)),
        ],
        compiler_params=pltpu.CompilerParams(
            collective_id=0, has_side_effects=True, vmem_limit_bytes=48 << 20
        ),
    )(adjoint, state, weights, vertical, mask, rate, neighbours, links, owners)


def solution(mesh):
    placed = (
        P("slab", None, "tiles", None),
        P("slab", None, "tiles", None),
        P("slab", "tiles", None),
        P("slab", "tiles", None),
        P("slab", "tiles", None),
        P(None, "tiles", None),
        P("tiles", None),
        P("tiles", None),
        P(),
    )
    return jax.shard_map(
        shards,
        mesh=mesh,
        in_specs=placed,
        out_specs=(P("slab", None, "tiles", None), P("slab", "tiles", None)),
        check_vma=False,
    )
```

```python
import jax
import jax.numpy as jnp
from jax import lax
from jax.experimental import pallas as pl
from jax.experimental.pallas import tpu as pltpu
from jax.sharding import PartitionSpec as P

TILE = 90
CELLS = TILE * TILE
BLOCK = 6
COARSE = 15
LANES = 128
ROWS = 64
LEVELS = 4
TRACERS = 3
FULL = LEVELS * ROWS
TAIL = CELLS - (ROWS - 1) * LANES
MESH = pl.DeviceIdType.MESH
FIELDS = 5
LAM = 2
GROUP = 7
NEAR = 8
FAR = 16


def iota(shape, dim):
    return lax.broadcasted_iota(jnp.int32, shape, dim)


def shifted(field, distance):
    rows = field.shape[0]
    lane = iota(field.shape, 1)
    down, over = divmod(distance, LANES)
    turned = pltpu.roll(field, (LANES - over) % LANES, 1)
    near = pltpu.roll(turned, (-down) % rows, 0) if down % rows else turned
    far = pltpu.roll(turned, (-down - 1) % rows, 0) if (down + 1) % rows else turned
    return jnp.where(lane >= LANES - over, far, near)


def pieces(value):
    high = value.astype(jnp.bfloat16)
    rest = value - high.astype(jnp.float32)
    middle = rest.astype(jnp.bfloat16)
    low = (rest - middle.astype(jnp.float32)).astype(jnp.bfloat16)
    return high, middle, low


def pick(value, onehot):
    high, middle, low = pieces(value)
    return (
        jnp.dot(high, onehot, preferred_element_type=jnp.float32)
        + jnp.dot(middle, onehot, preferred_element_type=jnp.float32)
        + jnp.dot(low, onehot, preferred_element_type=jnp.float32)
    )


def spread_rows(rows):
    return jnp.concatenate(
        [jnp.broadcast_to(rows[l : l + 1], (ROWS, LANES)) for l in range(LEVELS)], axis=0
    )


def kernel(
    adjoint, state, weights, vertical, mask, rate, neighbours, links, owners,
    out, gradient,
    adjoint_in, state_in, weights_in, vertical_in, mask_in, rate_in, neighbours_in, links_in,
    out_own, owners_in,
    mine, column, uptake, state_rows, inside, wet_rows, above_rows, below_rows, keep_rows,
    lam_rows, gather_side, mask_side, place_side, gather_block, mask_block,
    home_out, home_in, edge_out, edge_in, back_out, back_in, block_own, block_all, part, part_in,
    fetch, leave,
    send_field, recv_field, send_home, recv_home, send_edge, recv_edge, send_back, recv_back,
    send_near, recv_near, send_far, recv_far,
):
    here = lax.axis_index("tiles")
    slab = lax.axis_index("slab")
    tiles = lax.axis_size("tiles")
    core = here % 2
    depth = (here // 2) % 4
    across = (here // 8) % 4
    along = here // 32

    def slab_peer(k):
        return here, (slab + k) % LEVELS

    def beside(n):
        if n == 0:
            return (here + tiles - 2) % tiles, slab
        if n == 1:
            return (here + 2) % tiles, slab
        if n == 2:
            gone = (slab == 0).astype(jnp.int32)
            return (here + tiles - gone) % tiles, (slab + LEVELS - 1) % LEVELS
        gone = (slab == LEVELS - 1).astype(jnp.int32)
        return (here + gone) % tiles, (slab + 1) % LEVELS

    def home_peer(n):
        return (here + tiles + (-2, 2, -1, 1)[n]) % tiles, slab

    near_me = across * 2 + core
    far_me = along * 4 + depth

    def near_peer(k):
        other = (near_me + k) % NEAR
        return along * 32 + (other // 2) * 8 + depth * 2 + other % 2, slab

    def far_peer(k):
        other = (far_me + k) % FAR
        return (other // 4) * 32 + across * 8 + (other % 4) * 2 + core, slab

    arrays = (
        (mask, mask_in), (weights, weights_in), (vertical, vertical_in), (adjoint, adjoint_in),
        (rate, rate_in), (neighbours, neighbours_in), (links, links_in), (owners, owners_in),
        (state, state_in),
    )

    def fetched(a):
        return pltpu.make_async_copy(arrays[a][0], arrays[a][1], fetch.at[a])

    for a in range(len(arrays)):
        fetched(a).start()

    barrier = pltpu.get_barrier_semaphore()
    peers = (
        [slab_peer(k) for k in range(1, LEVELS)]
        + [home_peer(n) for n in range(4)]
        + [beside(n) for n in (2, 3)]
        + [near_peer(k) for k in range(1, NEAR)]
        + [far_peer(k) for k in range(1, FAR)]
    )
    for peer in peers:
        pl.semaphore_signal(barrier, inc=1, device_id=peer, device_id_type=MESH)

    small = iota((4, LANES), 1) < TAIL

    def last(ref, *lead):
        tail = ref[(*lead, slice(None), slice(CELLS - LANES, CELLS))]
        return jnp.where(small, pltpu.roll(tail, TAIL, 1), jnp.zeros_like(tail))

    def load_all(*jobs):
        def body(i, carry):
            for g in range(GROUP):
                k = i * GROUP + g
                at = pl.ds(pl.multiple_of(k * LANES, LANES), LANES)
                for start, read, _, target in jobs:
                    target[pl.ds(start + k, 4, stride=ROWS), :] = read(at)
            return carry

        lax.fori_loop(0, (ROWS - 1) // GROUP, body, 0)
        for start, _, read_last, target in jobs:
            target[pl.ds(start + ROWS - 1, 4, stride=ROWS), :] = read_last()

    def wet_of(value):
        return value.astype(jnp.float32)

    for a in range(4):
        fetched(a).wait()
    load_all(
        (
            0,
            lambda at: wet_of(mask_in[0, :, at]) * weights_in[0, :, at],
            lambda: wet_of(last(mask_in, 0)) * last(weights_in, 0),
            mine,
        ),
        (
            FULL,
            lambda at: wet_of(mask_in[0, :, at]) * vertical_in[0, :, at],
            lambda: wet_of(last(mask_in, 0)) * last(vertical_in, 0),
            mine,
        ),
        *[
            (
                (LAM + c) * FULL,
                lambda at, c=c: adjoint_in[0, c, :, at],
                lambda c=c: last(adjoint_in, 0, c),
                mine,
            )
            for c in range(TRACERS)
        ],
    )

    def row_of(f, which):
        return pl.ds(pl.multiple_of(f * FULL + which * ROWS, ROWS), ROWS)

    def field_copy(f, k):
        to = slab_peer(k)
        return pltpu.make_async_remote_copy(
            src_ref=mine.at[row_of(f, to[1])],
            dst_ref=column.at[row_of(f, slab)],
            send_sem=send_field.at[f, k],
            recv_sem=recv_field.at[f, k],
            device_id=to,
            device_id_type=MESH,
        )

    def send_field_on(f):
        for k in (2, 1, 3):
            field_copy(f, k).start()
        column[row_of(f, slab), :] = mine[row_of(f, slab), :]

    position = iota((LANES, 2 * LANES), 1)
    y = position % LANES
    cell = TILE * y + jnp.where(position < LANES, 0, TILE - 1)
    lane = iota((LANES, 2 * LANES), 0)
    gather_side[...] = ((cell % LANES == lane) & (y < TILE)).astype(jnp.bfloat16)
    position = iota((ROWS, 2 * LANES), 1)
    y = position % LANES
    cell = TILE * y + jnp.where(position < LANES, 0, TILE - 1)
    mask_side[...] = ((cell // LANES == iota((ROWS, 2 * LANES), 0)) & (y < TILE)).astype(jnp.float32)
    position = iota((2 * LANES, LANES), 0)
    y = position % LANES
    cell = TILE * y + jnp.where(position < LANES, 0, TILE - 1)
    place_side[...] = ((cell % LANES == iota((2 * LANES, LANES), 1)) & (y < TILE)).astype(jnp.bfloat16)
    position = iota((LANES, 2 * LANES), 1)
    cell = BLOCK * TILE * (position // COARSE) + BLOCK * (position % COARSE)
    gather_block[...] = (
        (cell % LANES == iota((LANES, 2 * LANES), 0)) & (position < COARSE * COARSE)
    ).astype(jnp.bfloat16)
    position = iota((ROWS, 2 * LANES), 1)
    cell = BLOCK * TILE * (position // COARSE) + BLOCK * (position % COARSE)
    mask_block[...] = (
        (cell // LANES == iota((ROWS, 2 * LANES), 0)) & (position < COARSE * COARSE)
    ).astype(jnp.float32)
    turn = (iota((LANES, LANES), 0) + iota((LANES, LANES), 1) == TILE - 1).astype(jnp.bfloat16)

    flat = (iota((FULL, LANES), 0) % ROWS) * LANES + iota((FULL, LANES), 1)
    in_row = flat % TILE
    first_row = flat < TILE
    final_row = flat >= CELLS - TILE
    inside[0:FULL] = (in_row != 0).astype(jnp.float32)
    inside[FULL : 2 * FULL] = (in_row != TILE - 1).astype(jnp.float32)

    fetched(5).wait()
    fetched(6).wait()

    def codes(to_all, link_all, tile):
        code, turned = [], []
        for side in range(4):
            to = jnp.broadcast_to(to_all[:, side : side + 1], (4, LANES))
            link = jnp.broadcast_to(link_all[:, side : side + 1], (4, LANES))
            slot = jnp.where(
                to == tile - 8, 0, jnp.where(to == tile + 8, 4, jnp.where(to == tile - 1, 8, 12))
            )
            code.append(jnp.where(to < 0, -1, slot + lax.shift_right_logical(link, 1)))
            turned.append((link & 1) == 1)
        return code, turned

    home_codes = codes(neighbours_in[...], links_in[...], here * 4 + iota((4, LANES), 0))

    lane4 = iota((LEVELS, LANES), 1)

    def edges_of(field):
        top = jnp.concatenate([field[l * ROWS : l * ROWS + 1] for l in range(LEVELS)], axis=0)
        one = jnp.concatenate([field[l * ROWS + 62 : l * ROWS + 63] for l in range(LEVELS)], axis=0)
        two = jnp.concatenate([field[l * ROWS + 63 : l * ROWS + 64] for l in range(LEVELS)], axis=0)
        low = jnp.where(lane4 < 54, pltpu.roll(one, 54, 1), pltpu.roll(two, 54, 1))
        sides = pick(field, gather_side[...])
        chosen = mask_side[...]
        rows = jnp.concatenate(
            [
                jnp.sum(sides[l * ROWS : (l + 1) * ROWS] * chosen, axis=0, keepdims=True)
                for l in range(LEVELS)
            ],
            axis=0,
        )
        return top, low, rows[:, :LANES], rows[:, LANES:]

    def edge_copy(m, n):
        return pltpu.make_async_remote_copy(
            src_ref=edge_out.at[m],
            dst_ref=edge_in.at[m, n ^ 1],
            send_sem=send_edge.at[m, n],
            recv_sem=recv_edge.at[m, n ^ 1],
            device_id=beside(n),
            device_id_type=MESH,
        )

    def home_copy(n):
        return pltpu.make_async_remote_copy(
            src_ref=home_out,
            dst_ref=home_in.at[n ^ 1],
            send_sem=send_home.at[n],
            recv_sem=recv_home.at[n ^ 1],
            device_id=home_peer(n),
            device_id_type=MESH,
        )

    def send_edges(m, field):
        for side, rows in enumerate(edges_of(field)):
            edge_out[m, side * LEVELS : (side + 1) * LEVELS, :] = rows
        for n in range(4):
            edge_copy(m, n).start()

    def home_edge(m, n, other):
        at = other * 4
        if n < 2:
            return home_in[n, m, at : at + 4, :]
        if n == 2:
            return jnp.concatenate([home_in[n, m, at + 3 : at + 4, :], home_out[m, at : at + 3, :]], axis=0)
        return jnp.concatenate([home_out[m, at + 1 : at + 4, :], home_in[n, m, at : at + 1, :]], axis=0)

    def halo(edge, which):
        code, turned = which
        found = [jnp.zeros((4, LANES), jnp.float32)] * 4
        for n in range(4):
            for other in range(4):
                value = edge(n, other)
                for side in range(4):
                    found[side] = jnp.where(code[side] == n * 4 + other, value, found[side])
        back = pick(jnp.concatenate(found, axis=0), turn)
        return [
            jnp.where(turned[side], back[side * LEVELS : (side + 1) * LEVELS], found[side])
            for side in range(4)
        ]

    def halo_home(m):
        return halo(lambda n, other: home_edge(m, n, other), home_codes)

    def halo_column(m):
        for n in range(4):
            edge_copy(m, n ^ 1).wait_recv()
        return halo(
            lambda n, other: edge_in[m, n, other * LEVELS : (other + 1) * LEVELS, :], column_codes
        )

    def neighbour_sum(field, sides):
        top, low, left, right = sides
        upper = jnp.where(first_row, spread_rows(top), shifted(field, -TILE))
        lower = jnp.where(final_row, spread_rows(pltpu.roll(low, 74, 1)), shifted(field, TILE))
        before = inside[0:FULL] * shifted(field, -1)
        after = inside[FULL : 2 * FULL] * shifted(field, 1)
        chosen = mask_side[...]
        both = jnp.concatenate([left, right], axis=1)
        placed = jnp.concatenate([chosen * both[l : l + 1] for l in range(LEVELS)], axis=0)
        return upper + lower + before + after + pick(placed, place_side[...])

    def arrived(f):
        for k in range(1, LEVELS):
            field_copy(f, k).wait_recv()

    def back_copy(c, k):
        to = slab_peer(k)
        return pltpu.make_async_remote_copy(
            src_ref=back_out.at[row_of(c, to[1])],
            dst_ref=back_in.at[row_of(c, slab)],
            send_sem=send_back.at[c, k],
            recv_sem=recv_back.at[c, k],
            device_id=to,
            device_id_type=MESH,
        )

    def couple(u):
        up = pltpu.roll(u, ROWS, 0)
        down = pltpu.roll(u, FULL - ROWS, 0)
        return u + above_rows[...] * (up - u) + below_rows[...] * (down - u)

    for c in range(TRACERS):
        lam = mine[(LAM + c) * FULL : (LAM + c + 1) * FULL]
        for side, rows in enumerate(edges_of(mine[0:FULL] * lam)):
            home_out[c, side * 4 : (side + 1) * 4, :] = rows
    for side, rows in enumerate(edges_of((mine[0:FULL] > 0).astype(jnp.float32))):
        home_out[TRACERS, side * 4 : (side + 1) * 4, :] = rows

    pl.semaphore_wait(barrier, len(peers))
    for n in range(4):
        home_copy(n).start()
    send_field_on(0)
    send_field_on(1)

    fetched(4).wait()
    load_all(
        *[
            (c * FULL, lambda at, c=c: 1.0 - rate_in[c, :, at], lambda c=c: 1.0 - last(rate_in, c), uptake)
            for c in range(TRACERS)
        ]
    )
    for n in range(4):
        home_copy(n ^ 1).wait_recv()
    wet = (mine[0:FULL] > 0).astype(jnp.float32)
    wet_rows[...] = wet
    keep_rows[...] = 1.0 - mine[0:FULL] * neighbour_sum(wet, halo_home(TRACERS))
    for c in range(TRACERS):
        lam = mine[(LAM + c) * FULL : (LAM + c + 1) * FULL]
        moved = lam * keep_rows[...] + wet_rows[...] * neighbour_sum(mine[0:FULL] * lam, halo_home(c))
        mine[(LAM + c) * FULL : (LAM + c + 1) * FULL] = moved * uptake[c * FULL : (c + 1) * FULL]
        send_field_on(LAM + c)

    column_codes = codes(
        jnp.broadcast_to(neighbours_in[pl.ds(slab, 1), :], (4, 4)),
        jnp.broadcast_to(links_in[pl.ds(slab, 1), :], (4, 4)),
        here * 4 + slab,
    )
    arrived(0)
    wet = (column[0:FULL] > 0).astype(jnp.float32)
    wet_rows[...] = wet
    send_edges(TRACERS, wet)
    arrived(1)
    inner = iota((FULL, LANES), 0) >= ROWS
    above = jnp.where(inner, column[FULL : 2 * FULL] * pltpu.roll(wet, ROWS, 0), 0.0)
    above_rows[...] = above
    below_rows[...] = pltpu.roll(above, FULL - ROWS, 0)

    def opens(c):
        arrived(LAM + c)
        at = pl.ds((LAM + c) * FULL, FULL)
        lam = couple(column[at, :])
        lam_rows[c * FULL : (c + 1) * FULL] = lam
        send_edges(c, column[0:FULL] * lam)

    def ends(c):
        lam = lam_rows[c * FULL : (c + 1) * FULL]
        moved = lam * keep_rows[...] + wet_rows[...] * neighbour_sum(column[0:FULL] * lam, halo_column(c))
        kept = uptake[row_of(c, slab), :]
        u = jnp.concatenate([moved[l * ROWS : (l + 1) * ROWS] * kept for l in range(LEVELS)], axis=0)
        back_out[c * FULL : (c + 1) * FULL] = couple(u)
        for k in (2, 1, 3):
            back_copy(c, k).start()
        back_in[row_of(c, slab), :] = back_out[row_of(c, slab), :]

    opens(0)
    keep_rows[...] = 1.0 - column[0:FULL] * neighbour_sum(wet_rows[...], halo_column(TRACERS))
    opens(1)
    ends(0)
    opens(2)
    ends(1)
    ends(2)

    fetched(7).wait()
    fetched(8).wait()
    block_own[...] = jnp.zeros_like(block_own)
    load_all(
        *[
            (c * FULL, lambda at, c=c: state_in[0, c, :, at], lambda c=c: last(state_in, 0, c), state_rows)
            for c in range(TRACERS)
        ]
    )

    def left(c):
        return pltpu.make_async_copy(out_own.at[c], out.at[0, c], leave.at[c])

    for c in range(TRACERS):
        for k in range(1, LEVELS):
            back_copy(c, k).wait_recv()

        def body(i, carry, c=c):
            for g in range(GROUP):
                k = i * GROUP + g
                out_own[c, :, pl.ds(pl.multiple_of(k * LANES, LANES), LANES)] = back_in[
                    pl.ds(c * FULL + k, 4, stride=ROWS), :
                ]
            return carry

        lax.fori_loop(0, (ROWS - 1) // GROUP, body, 0)
        out_own[c, :, (ROWS - 1) * LANES : CELLS] = back_in[
            pl.ds(c * FULL + ROWS - 1, 4, stride=ROWS), :
        ][:, :TAIL]
        left(c).start()
        lam = back_in[c * FULL : (c + 1) * FULL]
        term = jnp.where(mine[0:FULL] > 0, lam, 0.0) * state_rows[c * FULL : (c + 1) * FULL]
        three = term + shifted(term, 1) + shifted(term, 2)
        six = three + shifted(three, 3)
        three = six + shifted(six, TILE) + shifted(six, 2 * TILE)
        six = three + shifted(three, 3 * TILE)
        blocks = pick(six, gather_block[...])
        chosen = mask_block[...]
        for j in range(4):
            row = jnp.sum(blocks[j * ROWS : (j + 1) * ROWS] * chosen, axis=0, keepdims=True)
            block_own[8 * j + 2 * c : 8 * j + 2 * c + 1, :] = row[:, :LANES]
            block_own[8 * j + 2 * c + 1 : 8 * j + 2 * c + 2, :] = row[:, LANES:]

    def near_copy(k):
        return pltpu.make_async_remote_copy(
            src_ref=block_own,
            dst_ref=block_all.at[near_me],
            send_sem=send_near.at[k],
            recv_sem=recv_near.at[k],
            device_id=near_peer(k),
            device_id_type=MESH,
        )

    for k in range(1, NEAR):
        near_copy(k).start()
    block_all[near_me] = block_own[...]
    which = iota((8 * FAR, LANES), 0) // 8
    owner_of = (which // 4) * 32 + across * 8 + (which % 4) * 2 + core
    for k in range(1, NEAR):
        near_copy(k).wait_recv()

    def add(member, total):
        source = along * 32 + (member // 2) * 8 + depth * 2 + member % 2
        for j in range(4):
            owner = jnp.full((8 * FAR, LANES), owners_in[source * 4 + j], jnp.int32)
            rows = block_all[member, 8 * j : 8 * j + 8, :]
            total = total + jnp.where(owner == owner_of, jnp.concatenate([rows] * FAR, axis=0), 0.0)
        return total

    part[...] = lax.fori_loop(0, NEAR, add, jnp.zeros((8 * FAR, LANES), jnp.float32))

    def far_copy(k):
        other = (far_me + k) % FAR
        return pltpu.make_async_remote_copy(
            src_ref=part.at[pl.ds(pl.multiple_of(other * 8, 8), 8)],
            dst_ref=part_in.at[far_me],
            send_sem=send_far.at[k],
            recv_sem=recv_far.at[k],
            device_id=far_peer(k),
            device_id_type=MESH,
        )

    for k in range(1, FAR):
        far_copy(k).start()
    part_in[far_me] = part[pl.ds(pl.multiple_of(far_me * 8, 8), 8), :]
    for k in range(1, FAR):
        far_copy(k).wait_recv()
    total = part_in[0]
    for k in range(1, FAR):
        total = total + part_in[k]
    area = COARSE * COARSE
    for c in range(TRACERS):
        gradient[0, :, c * area : c * area + LANES] = total[2 * c : 2 * c + 1]
        gradient[0, :, c * area + LANES : (c + 1) * area] = total[2 * c + 1 : 2 * c + 2, : area - LANES]

    for f in range(FIELDS):
        for k in range(1, LEVELS):
            field_copy(f, k).wait_send()
    for n in range(4):
        home_copy(n).wait_send()
    for m in range(TRACERS + 1):
        for n in range(4):
            edge_copy(m, n).wait_send()
    for c in range(TRACERS):
        for k in range(1, LEVELS):
            back_copy(c, k).wait_send()
    for k in range(1, NEAR):
        near_copy(k).wait_send()
    for k in range(1, FAR):
        far_copy(k).wait_send()
    for c in range(TRACERS):
        left(c).wait()


def shards(adjoint, state, weights, vertical, mask, rate, neighbours, links, owners):
    vmem = pl.BlockSpec(memory_space=pltpu.VMEM)
    hbm = pl.BlockSpec(memory_space=pltpu.HBM)
    f32 = jnp.float32
    dma = pltpu.SemaphoreType.DMA
    held = [adjoint, state, weights, vertical, mask, rate, neighbours, links]
    edges = TRACERS + 1
    return pl.pallas_call(
        kernel,
        out_shape=(
            jax.ShapeDtypeStruct(adjoint.shape, f32),
            jax.ShapeDtypeStruct((1, 1, TRACERS * COARSE * COARSE), f32),
        ),
        in_specs=[hbm] * 9,
        out_specs=(hbm, vmem),
        scratch_shapes=[pltpu.VMEM(a.shape, a.dtype) for a in held]
        + [
            pltpu.VMEM(adjoint.shape[1:], f32),
            pltpu.SMEM(owners.shape, owners.dtype),
            pltpu.VMEM((FIELDS * FULL, LANES), f32),
            pltpu.VMEM((FIELDS * FULL, LANES), f32),
            pltpu.VMEM((TRACERS * FULL, LANES), f32),
            pltpu.VMEM((TRACERS * FULL, LANES), f32),
            pltpu.VMEM((2 * FULL, LANES), f32),
            pltpu.VMEM((FULL, LANES), f32),
            pltpu.VMEM((FULL, LANES), f32),
            pltpu.VMEM((FULL, LANES), f32),
            pltpu.VMEM((FULL, LANES), f32),
            pltpu.VMEM((TRACERS * FULL, LANES), f32),
            pltpu.VMEM((LANES, 2 * LANES), jnp.bfloat16),
            pltpu.VMEM((ROWS, 2 * LANES), f32),
            pltpu.VMEM((2 * LANES, LANES), jnp.bfloat16),
            pltpu.VMEM((LANES, 2 * LANES), jnp.bfloat16),
            pltpu.VMEM((ROWS, 2 * LANES), f32),
            pltpu.VMEM((edges, 16, LANES), f32),
            pltpu.VMEM((4, edges, 16, LANES), f32),
            pltpu.VMEM((edges, 16, LANES), f32),
            pltpu.VMEM((edges, 4, 16, LANES), f32),
            pltpu.VMEM((TRACERS * FULL, LANES), f32),
            pltpu.VMEM((TRACERS * FULL, LANES), f32),
            pltpu.VMEM((32, LANES), f32),
            pltpu.VMEM((NEAR, 32, LANES), f32),
            pltpu.VMEM((8 * FAR, LANES), f32),
            pltpu.VMEM((FAR, 8, LANES), f32),
            dma((9,)),
            dma((TRACERS,)),
            dma((FIELDS, LEVELS)),
            dma((FIELDS, LEVELS)),
            dma((4,)),
            dma((4,)),
            dma((edges, 4)),
            dma((edges, 4)),
            dma((TRACERS, LEVELS)),
            dma((TRACERS, LEVELS)),
            dma((NEAR,)),
            dma((NEAR,)),
            dma((FAR,)),
            dma((FAR,)),
        ],
        compiler_params=pltpu.CompilerParams(
            collective_id=0, has_side_effects=True, vmem_limit_bytes=64 << 20
        ),
    )(adjoint, state, weights, vertical, mask, rate, neighbours, links, owners)


def solution(mesh):
    placed = (
        P("slab", None, "tiles", None),
        P("slab", None, "tiles", None),
        P("slab", "tiles", None),
        P("slab", "tiles", None),
        P("slab", "tiles", None),
        P(None, "tiles", None),
        P("tiles", None),
        P("tiles", None),
        P(),
    )
    return jax.shard_map(
        shards,
        mesh=mesh,
        in_specs=placed,
        out_specs=(P("slab", None, "tiles", None), P("slab", "tiles", None)),
        check_vma=False,
    )
```

```python
import jax
import jax.numpy as jnp
from jax import lax
from jax.experimental import pallas as pl
from jax.experimental.pallas import tpu as pltpu
from jax.sharding import PartitionSpec as P

TILE = 90
CELLS = TILE * TILE
BLOCK = 6
COARSE = 15
LANES = 128
ROWS = 64
LEVELS = 4
TRACERS = 3
FULL = LEVELS * ROWS
TAIL = CELLS - (ROWS - 1) * LANES
MESH = pl.DeviceIdType.MESH
FIELDS = 5
LAM = 2
GROUP = 7
NEAR = 8
FAR = 16


def iota(shape, dim):
    return lax.broadcasted_iota(jnp.int32, shape, dim)


def shifted(field, distance):
    rows = field.shape[0]
    lane = iota(field.shape, 1)
    down, over = divmod(distance, LANES)
    turned = pltpu.roll(field, (LANES - over) % LANES, 1)
    near = pltpu.roll(turned, (-down) % rows, 0) if down % rows else turned
    far = pltpu.roll(turned, (-down - 1) % rows, 0) if (down + 1) % rows else turned
    return jnp.where(lane >= LANES - over, far, near)


def pieces(value):
    high = value.astype(jnp.bfloat16)
    rest = value - high.astype(jnp.float32)
    middle = rest.astype(jnp.bfloat16)
    low = (rest - middle.astype(jnp.float32)).astype(jnp.bfloat16)
    return high, middle, low


def pick(value, onehot):
    high, middle, low = pieces(value)
    return (
        jnp.dot(high, onehot, preferred_element_type=jnp.float32)
        + jnp.dot(middle, onehot, preferred_element_type=jnp.float32)
        + jnp.dot(low, onehot, preferred_element_type=jnp.float32)
    )


def spread_rows(rows):
    return jnp.concatenate(
        [jnp.broadcast_to(rows[l : l + 1], (ROWS, LANES)) for l in range(LEVELS)], axis=0
    )


def kernel(
    adjoint, state, weights, vertical, mask, rate, neighbours, links, owners,
    out, gradient,
    adjoint_in, state_in, weights_in, vertical_in, mask_in, rate_in, neighbours_in, links_in,
    out_own, owners_in,
    mine, column, uptake, state_rows, inside, wet_rows, above_rows, below_rows, keep_rows,
    lam_rows, gather_side, mask_side, place_side, gather_block, mask_block,
    home_out, home_in, wet_out, wet_in, edge_out, edge_in, back_out, back_in, block_own, block_all, part, part_in,
    fetch, leave,
    send_field, recv_field, send_home, recv_home, send_wet, recv_wet, send_edge, recv_edge, send_back, recv_back,
    send_near, recv_near, send_far, recv_far,
):
    here = lax.axis_index("tiles")
    slab = lax.axis_index("slab")
    tiles = lax.axis_size("tiles")
    core = here % 2
    depth = (here // 2) % 4
    across = (here // 8) % 4
    along = here // 32

    def slab_peer(k):
        return here, (slab + k) % LEVELS

    def beside(n):
        if n == 0:
            return (here + tiles - 2) % tiles, slab
        if n == 1:
            return (here + 2) % tiles, slab
        if n == 2:
            gone = (slab == 0).astype(jnp.int32)
            return (here + tiles - gone) % tiles, (slab + LEVELS - 1) % LEVELS
        gone = (slab == LEVELS - 1).astype(jnp.int32)
        return (here + gone) % tiles, (slab + 1) % LEVELS

    def home_peer(n):
        return (here + tiles + (-2, 2, -1, 1)[n]) % tiles, slab

    near_me = across * 2 + core
    far_me = along * 4 + depth

    def near_peer(k):
        other = (near_me + k) % NEAR
        return along * 32 + (other // 2) * 8 + depth * 2 + other % 2, slab

    def far_peer(k):
        other = (far_me + k) % FAR
        return (other // 4) * 32 + across * 8 + (other % 4) * 2 + core, slab

    arrays = (
        (mask, mask_in), (weights, weights_in), (vertical, vertical_in), (adjoint, adjoint_in),
        (rate, rate_in), (neighbours, neighbours_in), (links, links_in), (owners, owners_in),
        (state, state_in),
    )

    def fetched(a):
        return pltpu.make_async_copy(arrays[a][0], arrays[a][1], fetch.at[a])

    for a in range(len(arrays)):
        fetched(a).start()

    barrier = pltpu.get_barrier_semaphore()
    peers = (
        [slab_peer(k) for k in range(1, LEVELS)]
        + [home_peer(n) for n in range(4)]
        + [beside(n) for n in (2, 3)]
        + [near_peer(k) for k in range(1, NEAR)]
        + [far_peer(k) for k in range(1, FAR)]
    )
    for peer in peers:
        pl.semaphore_signal(barrier, inc=1, device_id=peer, device_id_type=MESH)

    small = iota((4, LANES), 1) < TAIL

    def last(ref, *lead):
        tail = ref[(*lead, slice(None), slice(CELLS - LANES, CELLS))]
        return jnp.where(small, pltpu.roll(tail, TAIL, 1), jnp.zeros_like(tail))

    def load_all(*jobs):
        def body(i, carry):
            for g in range(GROUP):
                k = i * GROUP + g
                at = pl.ds(pl.multiple_of(k * LANES, LANES), LANES)
                for start, read, _, target in jobs:
                    target[pl.ds(start + k, 4, stride=ROWS), :] = read(at)
            return carry

        lax.fori_loop(0, (ROWS - 1) // GROUP, body, 0)
        for start, _, read_last, target in jobs:
            target[pl.ds(start + ROWS - 1, 4, stride=ROWS), :] = read_last()

    def wet_of(value):
        return value.astype(jnp.float32)

    for a in range(4):
        fetched(a).wait()
    load_all(
        (
            0,
            lambda at: wet_of(mask_in[0, :, at]) * weights_in[0, :, at],
            lambda: wet_of(last(mask_in, 0)) * last(weights_in, 0),
            mine,
        ),
        (
            FULL,
            lambda at: wet_of(mask_in[0, :, at]) * vertical_in[0, :, at],
            lambda: wet_of(last(mask_in, 0)) * last(vertical_in, 0),
            mine,
        ),
        *[
            (
                (LAM + c) * FULL,
                lambda at, c=c: adjoint_in[0, c, :, at],
                lambda c=c: last(adjoint_in, 0, c),
                mine,
            )
            for c in range(TRACERS)
        ],
    )

    def row_of(f, which):
        return pl.ds(pl.multiple_of(f * FULL + which * ROWS, ROWS), ROWS)

    def field_copy(f, k):
        to = slab_peer(k)
        return pltpu.make_async_remote_copy(
            src_ref=mine.at[row_of(f, to[1])],
            dst_ref=column.at[row_of(f, slab)],
            send_sem=send_field.at[f, k],
            recv_sem=recv_field.at[f, k],
            device_id=to,
            device_id_type=MESH,
        )

    def send_field_on(f, order=(2, 1, 3)):
        for k in order:
            field_copy(f, k).start()

    def keep_own(f):
        column[row_of(f, slab), :] = mine[row_of(f, slab), :]

    position = iota((LANES, 2 * LANES), 1)
    y = position % LANES
    cell = TILE * y + jnp.where(position < LANES, 0, TILE - 1)
    lane = iota((LANES, 2 * LANES), 0)
    gather_side[...] = ((cell % LANES == lane) & (y < TILE)).astype(jnp.bfloat16)
    position = iota((ROWS, 2 * LANES), 1)
    y = position % LANES
    cell = TILE * y + jnp.where(position < LANES, 0, TILE - 1)
    mask_side[...] = ((cell // LANES == iota((ROWS, 2 * LANES), 0)) & (y < TILE)).astype(jnp.float32)
    position = iota((2 * LANES, LANES), 0)
    y = position % LANES
    cell = TILE * y + jnp.where(position < LANES, 0, TILE - 1)
    place_side[...] = ((cell % LANES == iota((2 * LANES, LANES), 1)) & (y < TILE)).astype(jnp.bfloat16)
    position = iota((LANES, 2 * LANES), 1)
    cell = BLOCK * TILE * (position // COARSE) + BLOCK * (position % COARSE)
    gather_block[...] = (
        (cell % LANES == iota((LANES, 2 * LANES), 0)) & (position < COARSE * COARSE)
    ).astype(jnp.bfloat16)
    position = iota((ROWS, 2 * LANES), 1)
    cell = BLOCK * TILE * (position // COARSE) + BLOCK * (position % COARSE)
    mask_block[...] = (
        (cell // LANES == iota((ROWS, 2 * LANES), 0)) & (position < COARSE * COARSE)
    ).astype(jnp.float32)
    turn = (iota((LANES, LANES), 0) + iota((LANES, LANES), 1) == TILE - 1).astype(jnp.bfloat16)

    flat = (iota((FULL, LANES), 0) % ROWS) * LANES + iota((FULL, LANES), 1)
    in_row = flat % TILE
    first_row = flat < TILE
    final_row = flat >= CELLS - TILE
    inside[0:FULL] = (in_row != 0).astype(jnp.float32)
    inside[FULL : 2 * FULL] = (in_row != TILE - 1).astype(jnp.float32)

    fetched(5).wait()
    fetched(6).wait()

    def codes(to_all, link_all, tile):
        code, turned = [], []
        for side in range(4):
            to = jnp.broadcast_to(to_all[:, side : side + 1], (4, LANES))
            link = jnp.broadcast_to(link_all[:, side : side + 1], (4, LANES))
            slot = jnp.where(
                to == tile - 8, 0, jnp.where(to == tile + 8, 4, jnp.where(to == tile - 1, 8, 12))
            )
            code.append(jnp.where(to < 0, -1, slot + lax.shift_right_logical(link, 1)))
            turned.append((link & 1) == 1)
        return code, turned

    home_codes = codes(neighbours_in[...], links_in[...], here * 4 + iota((4, LANES), 0))

    lane4 = iota((LEVELS, LANES), 1)

    def edges_of(field):
        top = jnp.concatenate([field[l * ROWS : l * ROWS + 1] for l in range(LEVELS)], axis=0)
        one = jnp.concatenate([field[l * ROWS + 62 : l * ROWS + 63] for l in range(LEVELS)], axis=0)
        two = jnp.concatenate([field[l * ROWS + 63 : l * ROWS + 64] for l in range(LEVELS)], axis=0)
        low = jnp.where(lane4 < 54, pltpu.roll(one, 54, 1), pltpu.roll(two, 54, 1))
        sides = pick(field, gather_side[...])
        chosen = mask_side[...]
        rows = jnp.concatenate(
            [
                jnp.sum(sides[l * ROWS : (l + 1) * ROWS] * chosen, axis=0, keepdims=True)
                for l in range(LEVELS)
            ],
            axis=0,
        )
        return top, low, rows[:, :LANES], rows[:, LANES:]

    def edge_copy(m, n):
        return pltpu.make_async_remote_copy(
            src_ref=edge_out.at[m],
            dst_ref=edge_in.at[m, n ^ 1],
            send_sem=send_edge.at[m, n],
            recv_sem=recv_edge.at[m, n ^ 1],
            device_id=beside(n),
            device_id_type=MESH,
        )

    def home_copy(n):
        return pltpu.make_async_remote_copy(
            src_ref=home_out,
            dst_ref=home_in.at[n ^ 1],
            send_sem=send_home.at[n],
            recv_sem=recv_home.at[n ^ 1],
            device_id=home_peer(n),
            device_id_type=MESH,
        )

    def wet_copy(k):
        to = slab_peer(k)
        return pltpu.make_async_remote_copy(
            src_ref=wet_out.at[to[1]],
            dst_ref=wet_in.at[slab],
            send_sem=send_wet.at[k],
            recv_sem=recv_wet.at[k],
            device_id=to,
            device_id_type=MESH,
        )

    left_over = LANES - TILE

    def send_edges(m, field):
        *three, fourth = edges_of(field)
        for side, rows in enumerate(three):
            rest = pltpu.roll(fourth, TILE - left_over * side, 1)
            edge_out[m, side * LEVELS : (side + 1) * LEVELS, :] = jnp.where(lane4 < TILE, rows, rest)
        for n in range(4):
            edge_copy(m, n).start()

    def home_edge(m, n, other):
        at = other * 4
        if n < 2:
            return home_in[n, m, at : at + 4, :]
        if n == 2:
            return jnp.concatenate([home_in[n, m, at + 3 : at + 4, :], home_out[m, at : at + 3, :]], axis=0)
        return jnp.concatenate([home_out[m, at + 1 : at + 4, :], home_in[n, m, at : at + 1, :]], axis=0)

    def halo(edge, which):
        code, turned = which
        found = [jnp.zeros((4, LANES), jnp.float32)] * 4
        for n in range(4):
            for other in range(4):
                value = edge(n, other)
                for side in range(4):
                    found[side] = jnp.where(code[side] == n * 4 + other, value, found[side])
        back = pick(jnp.concatenate(found, axis=0), turn)
        return [
            jnp.where(turned[side], back[side * LEVELS : (side + 1) * LEVELS], found[side])
            for side in range(4)
        ]

    def halo_home(m):
        return halo(lambda n, other: home_edge(m, n, other), home_codes)

    def halo_column(m):
        for n in range(4):
            edge_copy(m, n ^ 1).wait_recv()

        def edge(n, other):
            if other < 3:
                return edge_in[m, n, other * LEVELS : (other + 1) * LEVELS, :]
            parts = [
                pltpu.roll(edge_in[m, n, p * LEVELS : (p + 1) * LEVELS, :], left_over * (p + 1), 1)
                for p in range(3)
            ]
            return jnp.where(
                lane4 < left_over, parts[0], jnp.where(lane4 < 2 * left_over, parts[1], parts[2])
            )

        return halo(edge, column_codes)

    def neighbour_sum(field, sides):
        top, low, left, right = sides
        upper = jnp.where(first_row, spread_rows(top), shifted(field, -TILE))
        lower = jnp.where(final_row, spread_rows(pltpu.roll(low, 74, 1)), shifted(field, TILE))
        before = inside[0:FULL] * shifted(field, -1)
        after = inside[FULL : 2 * FULL] * shifted(field, 1)
        chosen = mask_side[...]
        both = jnp.concatenate([left, right], axis=1)
        placed = jnp.concatenate([chosen * both[l : l + 1] for l in range(LEVELS)], axis=0)
        return upper + lower + before + after + pick(placed, place_side[...])

    def arrived(f):
        for k in range(1, LEVELS):
            field_copy(f, k).wait_recv()

    def back_copy(c, k):
        to = slab_peer(k)
        return pltpu.make_async_remote_copy(
            src_ref=back_out.at[row_of(c, to[1])],
            dst_ref=back_in.at[row_of(c, slab)],
            send_sem=send_back.at[c, k],
            recv_sem=recv_back.at[c, k],
            device_id=to,
            device_id_type=MESH,
        )

    def couple(u):
        up = pltpu.roll(u, ROWS, 0)
        down = pltpu.roll(u, FULL - ROWS, 0)
        return u + above_rows[...] * (up - u) + below_rows[...] * (down - u)

    for c in range(TRACERS):
        lam = mine[(LAM + c) * FULL : (LAM + c + 1) * FULL]
        for side, rows in enumerate(edges_of(mine[0:FULL] * lam)):
            home_out[c, side * 4 : (side + 1) * 4, :] = rows
    for side, rows in enumerate(edges_of((mine[0:FULL] > 0).astype(jnp.float32))):
        home_out[TRACERS, side * 4 : (side + 1) * 4, :] = rows

    pl.semaphore_wait(barrier, len(peers))
    send_field_on(0)
    for n in range(4):
        home_copy(n).start()
    send_field_on(1)
    for f in range(2):
        keep_own(f)

    fetched(4).wait()
    load_all(
        *[
            (c * FULL, lambda at, c=c: 1.0 - rate_in[c, :, at], lambda c=c: 1.0 - last(rate_in, c), uptake)
            for c in range(TRACERS)
        ]
    )
    for n in range(4):
        home_copy(n ^ 1).wait_recv()
    wet = (mine[0:FULL] > 0).astype(jnp.float32)
    wet_rows[...] = wet
    sides = halo_home(TRACERS)
    for side in range(4):
        for j in range(4):
            wet_out[j, side : side + 1, :] = sides[side][j : j + 1]
    for k in (2, 1, 3):
        wet_copy(k).start()
    wet_in[slab] = wet_out[slab]
    keep_rows[...] = 1.0 - mine[0:FULL] * neighbour_sum(wet, sides)
    for c in range(TRACERS):
        lam = mine[(LAM + c) * FULL : (LAM + c + 1) * FULL]
        moved = lam * keep_rows[...] + wet_rows[...] * neighbour_sum(mine[0:FULL] * lam, halo_home(c))
        mine[(LAM + c) * FULL : (LAM + c + 1) * FULL] = moved * uptake[c * FULL : (c + 1) * FULL]
        send_field_on(LAM + c)
        keep_own(LAM + c)

    column_codes = codes(
        jnp.broadcast_to(neighbours_in[pl.ds(slab, 1), :], (4, 4)),
        jnp.broadcast_to(links_in[pl.ds(slab, 1), :], (4, 4)),
        here * 4 + slab,
    )
    arrived(0)
    wet = (column[0:FULL] > 0).astype(jnp.float32)
    wet_rows[...] = wet
    arrived(1)
    inner = iota((FULL, LANES), 0) >= ROWS
    above = jnp.where(inner, column[FULL : 2 * FULL] * pltpu.roll(wet, ROWS, 0), 0.0)
    above_rows[...] = above
    below_rows[...] = pltpu.roll(above, FULL - ROWS, 0)

    def opens(c):
        arrived(LAM + c)
        at = pl.ds((LAM + c) * FULL, FULL)
        lam = couple(column[at, :])
        lam_rows[c * FULL : (c + 1) * FULL] = lam
        send_edges(c, column[0:FULL] * lam)

    def ends(c):
        lam = lam_rows[c * FULL : (c + 1) * FULL]
        moved = lam * keep_rows[...] + wet_rows[...] * neighbour_sum(column[0:FULL] * lam, halo_column(c))
        kept = uptake[row_of(c, slab), :]
        u = jnp.concatenate([moved[l * ROWS : (l + 1) * ROWS] * kept for l in range(LEVELS)], axis=0)
        back_out[c * FULL : (c + 1) * FULL] = couple(u)
        for k in (2, 1, 3):
            back_copy(c, k).start()
        back_in[row_of(c, slab), :] = back_out[row_of(c, slab), :]

    for k in range(1, LEVELS):
        wet_copy(k).wait_recv()
    sides = [
        jnp.concatenate([wet_in[l, side : side + 1, :] for l in range(LEVELS)], axis=0)
        for side in range(4)
    ]
    keep_rows[...] = 1.0 - column[0:FULL] * neighbour_sum(wet_rows[...], sides)
    opens(0)
    opens(1)
    ends(0)
    opens(2)
    ends(1)
    ends(2)

    fetched(7).wait()
    fetched(8).wait()
    block_own[...] = jnp.zeros_like(block_own)
    load_all(
        *[
            (c * FULL, lambda at, c=c: state_in[0, c, :, at], lambda c=c: last(state_in, 0, c), state_rows)
            for c in range(TRACERS)
        ]
    )

    def left(c):
        return pltpu.make_async_copy(out_own.at[c], out.at[0, c], leave.at[c])

    for c in range(TRACERS):
        for k in range(1, LEVELS):
            back_copy(c, k).wait_recv()

        def body(i, carry, c=c):
            for g in range(GROUP):
                k = i * GROUP + g
                out_own[c, :, pl.ds(pl.multiple_of(k * LANES, LANES), LANES)] = back_in[
                    pl.ds(c * FULL + k, 4, stride=ROWS), :
                ]
            return carry

        lax.fori_loop(0, (ROWS - 1) // GROUP, body, 0)
        out_own[c, :, (ROWS - 1) * LANES : CELLS] = back_in[
            pl.ds(c * FULL + ROWS - 1, 4, stride=ROWS), :
        ][:, :TAIL]
        left(c).start()
        lam = back_in[c * FULL : (c + 1) * FULL]
        term = jnp.where(mine[0:FULL] > 0, lam, 0.0) * state_rows[c * FULL : (c + 1) * FULL]
        three = term + shifted(term, 1) + shifted(term, 2)
        six = three + shifted(three, 3)
        three = six + shifted(six, TILE) + shifted(six, 2 * TILE)
        six = three + shifted(three, 3 * TILE)
        blocks = pick(six, gather_block[...])
        chosen = mask_block[...]
        for j in range(4):
            row = jnp.sum(blocks[j * ROWS : (j + 1) * ROWS] * chosen, axis=0, keepdims=True)
            block_own[8 * j + 2 * c : 8 * j + 2 * c + 1, :] = row[:, :LANES]
            block_own[8 * j + 2 * c + 1 : 8 * j + 2 * c + 2, :] = row[:, LANES:]

    def near_copy(k):
        return pltpu.make_async_remote_copy(
            src_ref=block_own,
            dst_ref=block_all.at[near_me],
            send_sem=send_near.at[k],
            recv_sem=recv_near.at[k],
            device_id=near_peer(k),
            device_id_type=MESH,
        )

    for k in range(1, NEAR):
        near_copy(k).start()
    block_all[near_me] = block_own[...]
    which = iota((8 * FAR, LANES), 0) // 8
    owner_of = (which // 4) * 32 + across * 8 + (which % 4) * 2 + core
    for k in range(1, NEAR):
        near_copy(k).wait_recv()

    def add(member, total):
        source = along * 32 + (member // 2) * 8 + depth * 2 + member % 2
        for j in range(4):
            owner = jnp.full((8 * FAR, LANES), owners_in[source * 4 + j], jnp.int32)
            rows = block_all[member, 8 * j : 8 * j + 8, :]
            total = total + jnp.where(owner == owner_of, jnp.concatenate([rows] * FAR, axis=0), 0.0)
        return total

    part[...] = lax.fori_loop(0, NEAR, add, jnp.zeros((8 * FAR, LANES), jnp.float32))

    def far_copy(k):
        other = (far_me + k) % FAR
        return pltpu.make_async_remote_copy(
            src_ref=part.at[pl.ds(pl.multiple_of(other * 8, 8), 8)],
            dst_ref=part_in.at[far_me],
            send_sem=send_far.at[k],
            recv_sem=recv_far.at[k],
            device_id=far_peer(k),
            device_id_type=MESH,
        )

    for k in range(1, FAR):
        far_copy(k).start()
    part_in[far_me] = part[pl.ds(pl.multiple_of(far_me * 8, 8), 8), :]
    for k in range(1, FAR):
        far_copy(k).wait_recv()
    total = part_in[0]
    for k in range(1, FAR):
        total = total + part_in[k]
    area = COARSE * COARSE
    for c in range(TRACERS):
        gradient[0, :, c * area : c * area + LANES] = total[2 * c : 2 * c + 1]
        gradient[0, :, c * area + LANES : (c + 1) * area] = total[2 * c + 1 : 2 * c + 2, : area - LANES]

    for f in range(FIELDS):
        for k in range(1, LEVELS):
            field_copy(f, k).wait_send()
    for n in range(4):
        home_copy(n).wait_send()
    for k in range(1, LEVELS):
        wet_copy(k).wait_send()
    for m in range(TRACERS):
        for n in range(4):
            edge_copy(m, n).wait_send()
    for c in range(TRACERS):
        for k in range(1, LEVELS):
            back_copy(c, k).wait_send()
    for k in range(1, NEAR):
        near_copy(k).wait_send()
    for k in range(1, FAR):
        far_copy(k).wait_send()
    for c in range(TRACERS):
        left(c).wait()


def shards(adjoint, state, weights, vertical, mask, rate, neighbours, links, owners):
    vmem = pl.BlockSpec(memory_space=pltpu.VMEM)
    hbm = pl.BlockSpec(memory_space=pltpu.HBM)
    f32 = jnp.float32
    dma = pltpu.SemaphoreType.DMA
    held = [adjoint, state, weights, vertical, mask, rate, neighbours, links]
    edges = TRACERS + 1
    return pl.pallas_call(
        kernel,
        out_shape=(
            jax.ShapeDtypeStruct(adjoint.shape, f32),
            jax.ShapeDtypeStruct((1, 1, TRACERS * COARSE * COARSE), f32),
        ),
        in_specs=[hbm] * 9,
        out_specs=(hbm, vmem),
        scratch_shapes=[pltpu.VMEM(a.shape, a.dtype) for a in held]
        + [
            pltpu.VMEM(adjoint.shape[1:], f32),
            pltpu.SMEM(owners.shape, owners.dtype),
            pltpu.VMEM((FIELDS * FULL, LANES), f32),
            pltpu.VMEM((FIELDS * FULL, LANES), f32),
            pltpu.VMEM((TRACERS * FULL, LANES), f32),
            pltpu.VMEM((TRACERS * FULL, LANES), f32),
            pltpu.VMEM((2 * FULL, LANES), f32),
            pltpu.VMEM((FULL, LANES), f32),
            pltpu.VMEM((FULL, LANES), f32),
            pltpu.VMEM((FULL, LANES), f32),
            pltpu.VMEM((FULL, LANES), f32),
            pltpu.VMEM((TRACERS * FULL, LANES), f32),
            pltpu.VMEM((LANES, 2 * LANES), jnp.bfloat16),
            pltpu.VMEM((ROWS, 2 * LANES), f32),
            pltpu.VMEM((2 * LANES, LANES), jnp.bfloat16),
            pltpu.VMEM((LANES, 2 * LANES), jnp.bfloat16),
            pltpu.VMEM((ROWS, 2 * LANES), f32),
            pltpu.VMEM((edges, 16, LANES), f32),
            pltpu.VMEM((4, edges, 16, LANES), f32),
            pltpu.VMEM((4, 8, LANES), f32),
            pltpu.VMEM((LEVELS, 8, LANES), f32),
            pltpu.VMEM((TRACERS, 3 * LEVELS, LANES), f32),
            pltpu.VMEM((TRACERS, 4, 3 * LEVELS, LANES), f32),
            pltpu.VMEM((TRACERS * FULL, LANES), f32),
            pltpu.VMEM((TRACERS * FULL, LANES), f32),
            pltpu.VMEM((32, LANES), f32),
            pltpu.VMEM((NEAR, 32, LANES), f32),
            pltpu.VMEM((8 * FAR, LANES), f32),
            pltpu.VMEM((FAR, 8, LANES), f32),
            dma((9,)),
            dma((TRACERS,)),
            dma((FIELDS, LEVELS)),
            dma((FIELDS, LEVELS)),
            dma((4,)),
            dma((4,)),
            dma((LEVELS,)),
            dma((LEVELS,)),
            dma((TRACERS, 4)),
            dma((TRACERS, 4)),
            dma((TRACERS, LEVELS)),
            dma((TRACERS, LEVELS)),
            dma((NEAR,)),
            dma((NEAR,)),
            dma((FAR,)),
            dma((FAR,)),
        ],
        compiler_params=pltpu.CompilerParams(
            collective_id=0, has_side_effects=True, vmem_limit_bytes=64 << 20
        ),
    )(adjoint, state, weights, vertical, mask, rate, neighbours, links, owners)


def solution(mesh):
    placed = (
        P("slab", None, "tiles", None),
        P("slab", None, "tiles", None),
        P("slab", "tiles", None),
        P("slab", "tiles", None),
        P("slab", "tiles", None),
        P(None, "tiles", None),
        P("tiles", None),
        P("tiles", None),
        P(),
    )
    return jax.shard_map(
        shards,
        mesh=mesh,
        in_specs=placed,
        out_specs=(P("slab", None, "tiles", None), P("slab", "tiles", None)),
        check_vma=False,
    )
```

```python
import jax
import jax.numpy as jnp
from jax import lax
from jax.experimental import pallas as pl
from jax.experimental.pallas import tpu as pltpu
from jax.sharding import PartitionSpec as P

TILE = 90
CELLS = TILE * TILE
BLOCK = 6
COARSE = 15
LANES = 128
ROWS = 64
LEVELS = 4
TRACERS = 3
FULL = LEVELS * ROWS
TAIL = CELLS - (ROWS - 1) * LANES
MESH = pl.DeviceIdType.MESH
FIELDS = 5
LAM = 2
GROUP = 7
NEAR = 8
FAR = 16


def iota(shape, dim):
    return lax.broadcasted_iota(jnp.int32, shape, dim)


def shifted(field, distance):
    rows = field.shape[0]
    lane = iota(field.shape, 1)
    down, over = divmod(distance, LANES)
    turned = pltpu.roll(field, (LANES - over) % LANES, 1)
    near = pltpu.roll(turned, (-down) % rows, 0) if down % rows else turned
    far = pltpu.roll(turned, (-down - 1) % rows, 0) if (down + 1) % rows else turned
    return jnp.where(lane >= LANES - over, far, near)


def pieces(value):
    high = value.astype(jnp.bfloat16)
    rest = value - high.astype(jnp.float32)
    middle = rest.astype(jnp.bfloat16)
    low = (rest - middle.astype(jnp.float32)).astype(jnp.bfloat16)
    return high, middle, low


def pick(value, onehot):
    high, middle, low = pieces(value)
    return (
        jnp.dot(high, onehot, preferred_element_type=jnp.float32)
        + jnp.dot(middle, onehot, preferred_element_type=jnp.float32)
        + jnp.dot(low, onehot, preferred_element_type=jnp.float32)
    )


def spread_rows(rows):
    return jnp.concatenate(
        [jnp.broadcast_to(rows[l : l + 1], (ROWS, LANES)) for l in range(LEVELS)], axis=0
    )


def kernel(
    adjoint, state, weights, vertical, mask, rate, neighbours, links, owners,
    out, gradient,
    adjoint_in, state_in, weights_in, vertical_in, mask_in, rate_in, neighbours_in, links_in,
    out_own, owners_in,
    mine, column, uptake, state_rows, inside, wet_rows, above_rows, below_rows, keep_rows,
    lam_rows, gather_side, mask_side, place_side, gather_block, mask_block,
    home_out, home_in, end_out, end_in, wet_out, wet_in, edge_out, edge_in, back_out, back_in, block_own, block_all, part, part_in,
    fetch, leave,
    send_field, recv_field, send_home, recv_home, send_wet, recv_wet, send_edge, recv_edge, send_back, recv_back,
    send_near, recv_near, send_far, recv_far,
):
    here = lax.axis_index("tiles")
    slab = lax.axis_index("slab")
    tiles = lax.axis_size("tiles")
    core = here % 2
    depth = (here // 2) % 4
    across = (here // 8) % 4
    along = here // 32

    def slab_peer(k):
        return here, (slab + k) % LEVELS

    def beside(n):
        if n == 0:
            return (here + tiles - 2) % tiles, slab
        if n == 1:
            return (here + 2) % tiles, slab
        if n == 2:
            gone = (slab == 0).astype(jnp.int32)
            return (here + tiles - gone) % tiles, (slab + LEVELS - 1) % LEVELS
        gone = (slab == LEVELS - 1).astype(jnp.int32)
        return (here + gone) % tiles, (slab + 1) % LEVELS

    def home_peer(n):
        return (here + tiles + (-2, 2, -1, 1)[n]) % tiles, slab

    near_me = across * 2 + core
    far_me = along * 4 + depth

    def near_peer(k):
        other = (near_me + k) % NEAR
        return along * 32 + (other // 2) * 8 + depth * 2 + other % 2, slab

    def far_peer(k):
        other = (far_me + k) % FAR
        return (other // 4) * 32 + across * 8 + (other % 4) * 2 + core, slab

    arrays = (
        (mask, mask_in), (weights, weights_in), (vertical, vertical_in), (adjoint, adjoint_in),
        (rate, rate_in), (neighbours, neighbours_in), (links, links_in), (owners, owners_in),
        (state, state_in),
    )

    def fetched(a):
        return pltpu.make_async_copy(arrays[a][0], arrays[a][1], fetch.at[a])

    for a in range(len(arrays)):
        fetched(a).start()

    barrier = pltpu.get_barrier_semaphore()
    peers = (
        [slab_peer(k) for k in range(1, LEVELS)]
        + [home_peer(n) for n in range(4)]
        + [beside(n) for n in (2, 3)]
        + [near_peer(k) for k in range(1, NEAR)]
        + [far_peer(k) for k in range(1, FAR)]
    )
    for peer in peers:
        pl.semaphore_signal(barrier, inc=1, device_id=peer, device_id_type=MESH)

    small = iota((4, LANES), 1) < TAIL

    def last(ref, *lead):
        tail = ref[(*lead, slice(None), slice(CELLS - LANES, CELLS))]
        return jnp.where(small, pltpu.roll(tail, TAIL, 1), jnp.zeros_like(tail))

    def load_all(*jobs):
        def body(i, carry):
            for g in range(GROUP):
                k = i * GROUP + g
                at = pl.ds(pl.multiple_of(k * LANES, LANES), LANES)
                for start, read, _, target in jobs:
                    target[pl.ds(start + k, 4, stride=ROWS), :] = read(at)
            return carry

        lax.fori_loop(0, (ROWS - 1) // GROUP, body, 0)
        for start, _, read_last, target in jobs:
            target[pl.ds(start + ROWS - 1, 4, stride=ROWS), :] = read_last()

    def wet_of(value):
        return value.astype(jnp.float32)

    for a in range(4):
        fetched(a).wait()
    load_all(
        (
            0,
            lambda at: wet_of(mask_in[0, :, at]) * weights_in[0, :, at],
            lambda: wet_of(last(mask_in, 0)) * last(weights_in, 0),
            mine,
        ),
        (
            FULL,
            lambda at: wet_of(mask_in[0, :, at]) * vertical_in[0, :, at],
            lambda: wet_of(last(mask_in, 0)) * last(vertical_in, 0),
            mine,
        ),
        *[
            (
                (LAM + c) * FULL,
                lambda at, c=c: adjoint_in[0, c, :, at],
                lambda c=c: last(adjoint_in, 0, c),
                mine,
            )
            for c in range(TRACERS)
        ],
    )

    def row_of(f, which):
        return pl.ds(pl.multiple_of(f * FULL + which * ROWS, ROWS), ROWS)

    def field_copy(f, k):
        to = slab_peer(k)
        return pltpu.make_async_remote_copy(
            src_ref=mine.at[row_of(f, to[1])],
            dst_ref=column.at[row_of(f, slab)],
            send_sem=send_field.at[f, k],
            recv_sem=recv_field.at[f, k],
            device_id=to,
            device_id_type=MESH,
        )

    def send_field_on(f, order=(2, 1, 3)):
        for k in order:
            field_copy(f, k).start()

    def keep_own(f):
        column[row_of(f, slab), :] = mine[row_of(f, slab), :]

    position = iota((LANES, 2 * LANES), 1)
    y = position % LANES
    cell = TILE * y + jnp.where(position < LANES, 0, TILE - 1)
    lane = iota((LANES, 2 * LANES), 0)
    gather_side[...] = ((cell % LANES == lane) & (y < TILE)).astype(jnp.bfloat16)
    position = iota((ROWS, 2 * LANES), 1)
    y = position % LANES
    cell = TILE * y + jnp.where(position < LANES, 0, TILE - 1)
    mask_side[...] = ((cell // LANES == iota((ROWS, 2 * LANES), 0)) & (y < TILE)).astype(jnp.float32)
    position = iota((2 * LANES, LANES), 0)
    y = position % LANES
    cell = TILE * y + jnp.where(position < LANES, 0, TILE - 1)
    place_side[...] = ((cell % LANES == iota((2 * LANES, LANES), 1)) & (y < TILE)).astype(jnp.bfloat16)
    position = iota((LANES, 2 * LANES), 1)
    cell = BLOCK * TILE * (position // COARSE) + BLOCK * (position % COARSE)
    gather_block[...] = (
        (cell % LANES == iota((LANES, 2 * LANES), 0)) & (position < COARSE * COARSE)
    ).astype(jnp.bfloat16)
    position = iota((ROWS, 2 * LANES), 1)
    cell = BLOCK * TILE * (position // COARSE) + BLOCK * (position % COARSE)
    mask_block[...] = (
        (cell // LANES == iota((ROWS, 2 * LANES), 0)) & (position < COARSE * COARSE)
    ).astype(jnp.float32)
    turn = (iota((LANES, LANES), 0) + iota((LANES, LANES), 1) == TILE - 1).astype(jnp.bfloat16)

    flat = (iota((FULL, LANES), 0) % ROWS) * LANES + iota((FULL, LANES), 1)
    in_row = flat % TILE
    first_row = flat < TILE
    final_row = flat >= CELLS - TILE
    inside[0:FULL] = (in_row != 0).astype(jnp.float32)
    inside[FULL : 2 * FULL] = (in_row != TILE - 1).astype(jnp.float32)

    fetched(5).wait()
    fetched(6).wait()

    def codes(to_all, link_all, tile):
        code, turned = [], []
        for side in range(4):
            to = jnp.broadcast_to(to_all[:, side : side + 1], (4, LANES))
            link = jnp.broadcast_to(link_all[:, side : side + 1], (4, LANES))
            slot = jnp.where(
                to == tile - 8, 0, jnp.where(to == tile + 8, 4, jnp.where(to == tile - 1, 8, 12))
            )
            code.append(jnp.where(to < 0, -1, slot + lax.shift_right_logical(link, 1)))
            turned.append((link & 1) == 1)
        return code, turned

    home_codes = codes(neighbours_in[...], links_in[...], here * 4 + iota((4, LANES), 0))

    lane4 = iota((LEVELS, LANES), 1)

    def edges_of(field):
        top = jnp.concatenate([field[l * ROWS : l * ROWS + 1] for l in range(LEVELS)], axis=0)
        one = jnp.concatenate([field[l * ROWS + 62 : l * ROWS + 63] for l in range(LEVELS)], axis=0)
        two = jnp.concatenate([field[l * ROWS + 63 : l * ROWS + 64] for l in range(LEVELS)], axis=0)
        low = jnp.where(lane4 < 54, pltpu.roll(one, 54, 1), pltpu.roll(two, 54, 1))
        sides = pick(field, gather_side[...])
        chosen = mask_side[...]
        rows = jnp.concatenate(
            [
                jnp.sum(sides[l * ROWS : (l + 1) * ROWS] * chosen, axis=0, keepdims=True)
                for l in range(LEVELS)
            ],
            axis=0,
        )
        return top, low, rows[:, :LANES], rows[:, LANES:]

    def edge_copy(m, n):
        return pltpu.make_async_remote_copy(
            src_ref=edge_out.at[m],
            dst_ref=edge_in.at[m, n ^ 1],
            send_sem=send_edge.at[m, n],
            recv_sem=recv_edge.at[m, n ^ 1],
            device_id=beside(n),
            device_id_type=MESH,
        )

    def keep_edge(m, side, rows):
        home_out[m, side * 4 : (side + 1) * 4, :] = rows
        at = m * 4 + side
        end_out[0, at : at + 1, :] = rows[0:1]
        end_out[1, at : at + 1, :] = rows[3:4]

    def home_copy(n):
        return pltpu.make_async_remote_copy(
            src_ref=home_out if n < 2 else end_out.at[n - 2],
            dst_ref=home_in.at[n ^ 1] if n < 2 else end_in.at[(n ^ 1) - 2],
            send_sem=send_home.at[n],
            recv_sem=recv_home.at[n ^ 1],
            device_id=home_peer(n),
            device_id_type=MESH,
        )

    def wet_copy(k):
        to = slab_peer(k)
        return pltpu.make_async_remote_copy(
            src_ref=wet_out.at[to[1]],
            dst_ref=wet_in.at[slab],
            send_sem=send_wet.at[k],
            recv_sem=recv_wet.at[k],
            device_id=to,
            device_id_type=MESH,
        )

    left_over = LANES - TILE

    def send_edges(m, field):
        *three, fourth = edges_of(field)
        for side, rows in enumerate(three):
            rest = pltpu.roll(fourth, TILE - left_over * side, 1)
            edge_out[m, side * LEVELS : (side + 1) * LEVELS, :] = jnp.where(lane4 < TILE, rows, rest)
        for n in range(4):
            edge_copy(m, n).start()

    def home_edge(m, n, other):
        at = other * 4
        if n < 2:
            return home_in[n, m, at : at + 4, :]
        if n == 2:
            return jnp.concatenate([end_in[0, m * 4 + other : m * 4 + other + 1, :], home_out[m, at : at + 3, :]], axis=0)
        return jnp.concatenate([home_out[m, at + 1 : at + 4, :], end_in[1, m * 4 + other : m * 4 + other + 1, :]], axis=0)

    def halo(edge, which):
        code, turned = which
        found = [jnp.zeros((4, LANES), jnp.float32)] * 4
        for n in range(4):
            for other in range(4):
                value = edge(n, other)
                for side in range(4):
                    found[side] = jnp.where(code[side] == n * 4 + other, value, found[side])
        back = pick(jnp.concatenate(found, axis=0), turn)
        return [
            jnp.where(turned[side], back[side * LEVELS : (side + 1) * LEVELS], found[side])
            for side in range(4)
        ]

    def halo_home(m):
        return halo(lambda n, other: home_edge(m, n, other), home_codes)

    def halo_column(m):
        for n in range(4):
            edge_copy(m, n ^ 1).wait_recv()

        def edge(n, other):
            if other < 3:
                return edge_in[m, n, other * LEVELS : (other + 1) * LEVELS, :]
            parts = [
                pltpu.roll(edge_in[m, n, p * LEVELS : (p + 1) * LEVELS, :], left_over * (p + 1), 1)
                for p in range(3)
            ]
            return jnp.where(
                lane4 < left_over, parts[0], jnp.where(lane4 < 2 * left_over, parts[1], parts[2])
            )

        return halo(edge, column_codes)

    def neighbour_sum(field, sides):
        top, low, left, right = sides
        upper = jnp.where(first_row, spread_rows(top), shifted(field, -TILE))
        lower = jnp.where(final_row, spread_rows(pltpu.roll(low, 74, 1)), shifted(field, TILE))
        before = inside[0:FULL] * shifted(field, -1)
        after = inside[FULL : 2 * FULL] * shifted(field, 1)
        chosen = mask_side[...]
        both = jnp.concatenate([left, right], axis=1)
        placed = jnp.concatenate([chosen * both[l : l + 1] for l in range(LEVELS)], axis=0)
        return upper + lower + before + after + pick(placed, place_side[...])

    def arrived(f):
        for k in range(1, LEVELS):
            field_copy(f, k).wait_recv()

    def back_copy(c, k):
        to = slab_peer(k)
        return pltpu.make_async_remote_copy(
            src_ref=back_out.at[row_of(c, to[1])],
            dst_ref=back_in.at[row_of(c, slab)],
            send_sem=send_back.at[c, k],
            recv_sem=recv_back.at[c, k],
            device_id=to,
            device_id_type=MESH,
        )

    def couple(u):
        up = pltpu.roll(u, ROWS, 0)
        down = pltpu.roll(u, FULL - ROWS, 0)
        return u + above_rows[...] * (up - u) + below_rows[...] * (down - u)

    for c in range(TRACERS):
        lam = mine[(LAM + c) * FULL : (LAM + c + 1) * FULL]
        for side, rows in enumerate(edges_of(mine[0:FULL] * lam)):
            keep_edge(c, side, rows)
    for side, rows in enumerate(edges_of((mine[0:FULL] > 0).astype(jnp.float32))):
        keep_edge(TRACERS, side, rows)

    pl.semaphore_wait(barrier, len(peers))
    send_field_on(0)
    for n in range(4):
        home_copy(n).start()
    send_field_on(1)
    for f in range(2):
        keep_own(f)

    fetched(4).wait()
    load_all(
        *[
            (c * FULL, lambda at, c=c: 1.0 - rate_in[c, :, at], lambda c=c: 1.0 - last(rate_in, c), uptake)
            for c in range(TRACERS)
        ]
    )
    for n in range(4):
        home_copy(n ^ 1).wait_recv()
    wet = (mine[0:FULL] > 0).astype(jnp.float32)
    wet_rows[...] = wet
    sides = halo_home(TRACERS)
    for side in range(4):
        for j in range(4):
            wet_out[j, side : side + 1, :] = sides[side][j : j + 1]
    for k in (2, 1, 3):
        wet_copy(k).start()
    wet_in[slab] = wet_out[slab]
    keep_rows[...] = 1.0 - mine[0:FULL] * neighbour_sum(wet, sides)
    for c in range(TRACERS):
        lam = mine[(LAM + c) * FULL : (LAM + c + 1) * FULL]
        moved = lam * keep_rows[...] + wet_rows[...] * neighbour_sum(mine[0:FULL] * lam, halo_home(c))
        mine[(LAM + c) * FULL : (LAM + c + 1) * FULL] = moved * uptake[c * FULL : (c + 1) * FULL]
        send_field_on(LAM + c)
        keep_own(LAM + c)

    column_codes = codes(
        jnp.broadcast_to(neighbours_in[pl.ds(slab, 1), :], (4, 4)),
        jnp.broadcast_to(links_in[pl.ds(slab, 1), :], (4, 4)),
        here * 4 + slab,
    )
    arrived(0)
    wet = (column[0:FULL] > 0).astype(jnp.float32)
    wet_rows[...] = wet
    arrived(1)
    inner = iota((FULL, LANES), 0) >= ROWS
    above = jnp.where(inner, column[FULL : 2 * FULL] * pltpu.roll(wet, ROWS, 0), 0.0)
    above_rows[...] = above
    below_rows[...] = pltpu.roll(above, FULL - ROWS, 0)

    def opens(c):
        arrived(LAM + c)
        at = pl.ds((LAM + c) * FULL, FULL)
        lam = couple(column[at, :])
        lam_rows[c * FULL : (c + 1) * FULL] = lam
        send_edges(c, column[0:FULL] * lam)

    def ends(c):
        lam = lam_rows[c * FULL : (c + 1) * FULL]
        moved = lam * keep_rows[...] + wet_rows[...] * neighbour_sum(column[0:FULL] * lam, halo_column(c))
        kept = uptake[row_of(c, slab), :]
        u = jnp.concatenate([moved[l * ROWS : (l + 1) * ROWS] * kept for l in range(LEVELS)], axis=0)
        back_out[c * FULL : (c + 1) * FULL] = couple(u)
        for k in (2, 1, 3):
            back_copy(c, k).start()
        back_in[row_of(c, slab), :] = back_out[row_of(c, slab), :]

    for k in range(1, LEVELS):
        wet_copy(k).wait_recv()
    sides = [
        jnp.concatenate([wet_in[l, side : side + 1, :] for l in range(LEVELS)], axis=0)
        for side in range(4)
    ]
    keep_rows[...] = 1.0 - column[0:FULL] * neighbour_sum(wet_rows[...], sides)
    opens(0)
    opens(1)
    ends(0)
    opens(2)
    ends(1)
    ends(2)

    fetched(7).wait()
    fetched(8).wait()
    block_own[...] = jnp.zeros_like(block_own)
    load_all(
        *[
            (c * FULL, lambda at, c=c: state_in[0, c, :, at], lambda c=c: last(state_in, 0, c), state_rows)
            for c in range(TRACERS)
        ]
    )

    def left(c):
        return pltpu.make_async_copy(out_own.at[c], out.at[0, c], leave.at[c])

    def give(c):
        def body(i, carry):
            for g in range(GROUP):
                k = i * GROUP + g
                out_own[c, :, pl.ds(pl.multiple_of(k * LANES, LANES), LANES)] = back_in[
                    pl.ds(c * FULL + k, 4, stride=ROWS), :
                ]
            return carry

        lax.fori_loop(0, (ROWS - 1) // GROUP, body, 0)
        out_own[c, :, (ROWS - 1) * LANES : CELLS] = back_in[
            pl.ds(c * FULL + ROWS - 1, 4, stride=ROWS), :
        ][:, :TAIL]
        left(c).start()

    for c in range(TRACERS):
        for k in range(1, LEVELS):
            back_copy(c, k).wait_recv()

        if c < TRACERS - 1:
            give(c)
        lam = back_in[c * FULL : (c + 1) * FULL]
        term = jnp.where(mine[0:FULL] > 0, lam, 0.0) * state_rows[c * FULL : (c + 1) * FULL]
        three = term + shifted(term, 1) + shifted(term, 2)
        six = three + shifted(three, 3)
        three = six + shifted(six, TILE) + shifted(six, 2 * TILE)
        six = three + shifted(three, 3 * TILE)
        blocks = pick(six, gather_block[...])
        chosen = mask_block[...]
        for j in range(4):
            row = jnp.sum(blocks[j * ROWS : (j + 1) * ROWS] * chosen, axis=0, keepdims=True)
            block_own[8 * j + 2 * c : 8 * j + 2 * c + 1, :] = row[:, :LANES]
            block_own[8 * j + 2 * c + 1 : 8 * j + 2 * c + 2, :] = row[:, LANES:]

    def near_copy(k):
        return pltpu.make_async_remote_copy(
            src_ref=block_own,
            dst_ref=block_all.at[near_me],
            send_sem=send_near.at[k],
            recv_sem=recv_near.at[k],
            device_id=near_peer(k),
            device_id_type=MESH,
        )

    for k in range(1, NEAR):
        near_copy(k).start()
    block_all[near_me] = block_own[...]
    give(TRACERS - 1)
    which = iota((8 * FAR, LANES), 0) // 8
    owner_of = (which // 4) * 32 + across * 8 + (which % 4) * 2 + core
    for k in range(1, NEAR):
        near_copy(k).wait_recv()

    def add(member, total):
        source = along * 32 + (member // 2) * 8 + depth * 2 + member % 2
        for j in range(4):
            owner = jnp.full((8 * FAR, LANES), owners_in[source * 4 + j], jnp.int32)
            rows = block_all[member, 8 * j : 8 * j + 8, :]
            total = total + jnp.where(owner == owner_of, jnp.concatenate([rows] * FAR, axis=0), 0.0)
        return total

    part[...] = lax.fori_loop(0, NEAR, add, jnp.zeros((8 * FAR, LANES), jnp.float32))

    def far_copy(k):
        other = (far_me + k) % FAR
        return pltpu.make_async_remote_copy(
            src_ref=part.at[pl.ds(pl.multiple_of(other * 8, 8), 8)],
            dst_ref=part_in.at[far_me],
            send_sem=send_far.at[k],
            recv_sem=recv_far.at[k],
            device_id=far_peer(k),
            device_id_type=MESH,
        )

    for k in range(1, FAR):
        far_copy(k).start()
    part_in[far_me] = part[pl.ds(pl.multiple_of(far_me * 8, 8), 8), :]
    for k in range(1, FAR):
        far_copy(k).wait_recv()
    total = part_in[0]
    for k in range(1, FAR):
        total = total + part_in[k]
    area = COARSE * COARSE
    for c in range(TRACERS):
        gradient[0, :, c * area : c * area + LANES] = total[2 * c : 2 * c + 1]
        gradient[0, :, c * area + LANES : (c + 1) * area] = total[2 * c + 1 : 2 * c + 2, : area - LANES]

    for f in range(FIELDS):
        for k in range(1, LEVELS):
            field_copy(f, k).wait_send()
    for n in range(4):
        home_copy(n).wait_send()
    for k in range(1, LEVELS):
        wet_copy(k).wait_send()
    for m in range(TRACERS):
        for n in range(4):
            edge_copy(m, n).wait_send()
    for c in range(TRACERS):
        for k in range(1, LEVELS):
            back_copy(c, k).wait_send()
    for k in range(1, NEAR):
        near_copy(k).wait_send()
    for k in range(1, FAR):
        far_copy(k).wait_send()
    for c in range(TRACERS):
        left(c).wait()


def shards(adjoint, state, weights, vertical, mask, rate, neighbours, links, owners):
    vmem = pl.BlockSpec(memory_space=pltpu.VMEM)
    hbm = pl.BlockSpec(memory_space=pltpu.HBM)
    f32 = jnp.float32
    dma = pltpu.SemaphoreType.DMA
    held = [adjoint, state, weights, vertical, mask, rate, neighbours, links]
    edges = TRACERS + 1
    return pl.pallas_call(
        kernel,
        out_shape=(
            jax.ShapeDtypeStruct(adjoint.shape, f32),
            jax.ShapeDtypeStruct((1, 1, TRACERS * COARSE * COARSE), f32),
        ),
        in_specs=[hbm] * 9,
        out_specs=(hbm, vmem),
        scratch_shapes=[pltpu.VMEM(a.shape, a.dtype) for a in held]
        + [
            pltpu.VMEM(adjoint.shape[1:], f32),
            pltpu.SMEM(owners.shape, owners.dtype),
            pltpu.VMEM((FIELDS * FULL, LANES), f32),
            pltpu.VMEM((FIELDS * FULL, LANES), f32),
            pltpu.VMEM((TRACERS * FULL, LANES), f32),
            pltpu.VMEM((TRACERS * FULL, LANES), f32),
            pltpu.VMEM((2 * FULL, LANES), f32),
            pltpu.VMEM((FULL, LANES), f32),
            pltpu.VMEM((FULL, LANES), f32),
            pltpu.VMEM((FULL, LANES), f32),
            pltpu.VMEM((FULL, LANES), f32),
            pltpu.VMEM((TRACERS * FULL, LANES), f32),
            pltpu.VMEM((LANES, 2 * LANES), jnp.bfloat16),
            pltpu.VMEM((ROWS, 2 * LANES), f32),
            pltpu.VMEM((2 * LANES, LANES), jnp.bfloat16),
            pltpu.VMEM((LANES, 2 * LANES), jnp.bfloat16),
            pltpu.VMEM((ROWS, 2 * LANES), f32),
            pltpu.VMEM((edges, 16, LANES), f32),
            pltpu.VMEM((2, edges, 16, LANES), f32),
            pltpu.VMEM((2, 16, LANES), f32),
            pltpu.VMEM((2, 16, LANES), f32),
            pltpu.VMEM((4, 8, LANES), f32),
            pltpu.VMEM((LEVELS, 8, LANES), f32),
            pltpu.VMEM((TRACERS, 3 * LEVELS, LANES), f32),
            pltpu.VMEM((TRACERS, 4, 3 * LEVELS, LANES), f32),
            pltpu.VMEM((TRACERS * FULL, LANES), f32),
            pltpu.VMEM((TRACERS * FULL, LANES), f32),
            pltpu.VMEM((32, LANES), f32),
            pltpu.VMEM((NEAR, 32, LANES), f32),
            pltpu.VMEM((8 * FAR, LANES), f32),
            pltpu.VMEM((FAR, 8, LANES), f32),
            dma((9,)),
            dma((TRACERS,)),
            dma((FIELDS, LEVELS)),
            dma((FIELDS, LEVELS)),
            dma((4,)),
            dma((4,)),
            dma((LEVELS,)),
            dma((LEVELS,)),
            dma((TRACERS, 4)),
            dma((TRACERS, 4)),
            dma((TRACERS, LEVELS)),
            dma((TRACERS, LEVELS)),
            dma((NEAR,)),
            dma((NEAR,)),
            dma((FAR,)),
            dma((FAR,)),
        ],
        compiler_params=pltpu.CompilerParams(
            collective_id=0, has_side_effects=True, vmem_limit_bytes=64 << 20
        ),
    )(adjoint, state, weights, vertical, mask, rate, neighbours, links, owners)


def solution(mesh):
    placed = (
        P("slab", None, "tiles", None),
        P("slab", None, "tiles", None),
        P("slab", "tiles", None),
        P("slab", "tiles", None),
        P("slab", "tiles", None),
        P(None, "tiles", None),
        P("tiles", None),
        P("tiles", None),
        P(),
    )
    return jax.shard_map(
        shards,
        mesh=mesh,
        in_specs=placed,
        out_specs=(P("slab", None, "tiles", None), P("slab", "tiles", None)),
        check_vma=False,
    )
```
